256 devices in a mesh: row: 16 (over z, core), col: 16 (over y, x).
Axes of the slice: x: 4, y: 4, z: 8, core: 2. Of those that a mesh axis runs over, the one named last changes fastest.
Arguments:
- hessian_inverse: float32 [6656, 6656], P('row', 'col'), may hold values from -9 to 13, as said below
- weights: bfloat16 [32768, 6656], P('row', 'col'), may hold values from -6 to 6
- pruned: int32 [512], replicated, may hold values from 0 to 6655, as said below
Outputs:
- inverse_updated: float32 [6656, 6656], P('row', 'col')
- weights_updated: float32 [32768, 6656], P('row', 'col')
The draws below stay inside these ranges and needn't reach their ends.
Inputs may be any that keep to these rules, and one draw needn't show every extreme that they name: `pruned`: 512 distinct hidden units in increasing order; at most 64 of them fall in one column tile of 416 consecutive units, and exactly 64 in some tile. `hessian_inverse`: symmetric positive definite.
All inputs are finite; a program needn't handle non-finite values.
Results may differ from the reference program's by a relative error of at most 0.0003.
Values may be sent and summed in bfloat16 or wider, within the bound.
No kernel may reach another device: no remote copies, remote signals or barrier semaphores. Data moves between devices by JAX's collectives and lax.ppermute only.
A program may use at most 128 MiB of HBM per device.

```python
import math
import jax
import jax.numpy as jnp
from jax import lax

H = 6656
K = 512
ROWS = 32768
COL_TILES = 16
CAP = 64


shared_rank = 32


common_weight = 2.0


def draw_hessian_inverse(key, part):
    first, second, third = jax.random.split(jax.random.fold_in(key, 23), 3)
    noise = jax.random.truncated_normal(first, -4.0, 4.0, (H, H), jnp.float32)
    symmetric = (jnp.triu(noise) + jnp.triu(noise, 1).T) * (0.4 / math.sqrt(H))
    factors = jax.random.normal(second, (H, shared_rank), jnp.float32)
    lengths = jnp.sqrt(jnp.sum(factors * factors, axis=1, keepdims=True) / shared_rank + 1e-06)
    factors = factors / lengths
    common = jnp.dot(factors, factors.T, precision=lax.Precision.HIGHEST) / shared_rank
    core = jnp.eye(H, dtype=jnp.float32) + symmetric + common_weight * common
    logs = jax.random.uniform(third, (H,), jnp.float32, math.log(0.3), math.log(3.0))
    roots = jnp.exp(0.5 * logs)
    return roots[:, None] * core * roots[None, :]


def draw_pruned(key, part):
    width = H // COL_TILES
    first, second, third = jax.random.split(jax.random.fold_in(key, 11), 3)
    boost = jax.random.randint(first, (COL_TILES,), 0, 4)
    heavy = jax.random.randint(second, (), 0, COL_TILES)
    boost = jnp.where(jnp.arange(COL_TILES) == heavy, 4, boost)
    noise = jax.random.randint(third, (COL_TILES, width), 0, 1024)
    score = (boost[:, None] * 1024 + noise) * H + jnp.arange(H, dtype=jnp.int32).reshape(COL_TILES, width)
    cutoff = lax.top_k(score, CAP)[0][:, CAP - 1]
    score = jnp.where(score >= cutoff[:, None], score, -1).reshape(H)
    chosen = lax.top_k(score, K)[1]
    return jnp.sort(chosen).astype(jnp.int32)


def shard_levels(own_key, extent, pieces, smallest, high):
    def one(axis_at, shards_of):
        draws = jax.random.uniform(jax.random.fold_in(jax.random.fold_in(own_key, 6), axis_at), (shards_of,), jnp.float32, smallest / len(pieces), high / len(pieces))
        return jnp.repeat(jnp.exp(draws), extent[axis_at] // shards_of).reshape((-1,) + (1,) * (len(extent) - axis_at - 1))

    loudness = one(*pieces[0])
    for cut in pieces[1:]:
        loudness = loudness * one(*cut)
    return loudness


def centred(key, extent, deviation, most, pieces=(), held_as=jnp.bfloat16):
    values = deviation * jax.random.normal(key, extent, jnp.float32)
    if pieces:
        values = values * shard_levels(key, extent, pieces, -0.22, 0.18)
    return jnp.clip(values, -most, most).astype(held_as)


def setup_inputs(seed: int = 0) -> dict:
    key_list = jax.random.split(jax.random.key(seed), 4)
    return {
        "hessian_inverse": draw_hessian_inverse(jax.random.fold_in(key_list[3], 71), 0),
        "weights": centred(key_list[1], (ROWS, H), 1.0, 6.0, ((0, 16), (1, 16))),
        "pruned": draw_pruned(jax.random.fold_in(key_list[3], 71), 0),
    }


def reference(hessian_inverse, weights, pruned):
    high = lax.Precision.HIGHEST
    panel = jnp.take(hessian_inverse, pruned, axis=0)
    block = jnp.take(panel, pruned, axis=1)
    inverse_cols = jnp.take(hessian_inverse, pruned, axis=1)
    weight_cols = jnp.take(weights, pruned, axis=1).astype(jnp.float32)
    factor = jnp.linalg.cholesky(block)
    solved = jax.scipy.linalg.cho_solve((factor, True), panel)
    inverse_updated = hessian_inverse - jnp.dot(inverse_cols, solved, precision=high)
    hit = jnp.zeros((hessian_inverse.shape[0],), jnp.float32).at[pruned].set(1.0)
    keep = 1.0 - hit
    weights_updated = (weights.astype(jnp.float32) - jnp.dot(weight_cols, solved, precision=high)) * keep[None, :]
    return (inverse_updated, weights_updated)
```

```python
import jax
import jax.numpy as jnp
from jax import lax
from jax.experimental import pallas as pl
from jax.experimental.pallas import tpu as pltpu
from jax.sharding import PartitionSpec as P

HIGH = lax.Precision.HIGHEST
F32 = jnp.float32
BF16 = jnp.bfloat16
VMEM = pl.BlockSpec(memory_space=pltpu.VMEM)
SMEM = pl.BlockSpec(memory_space=pltpu.SMEM)
BASE = 128


def across(a, b, dims, precision=None):
    return lax.dot_general(a, b, (dims, ((), ())), precision=precision, preferred_element_type=F32)


def one_hot(index, width):
    slots = index.shape[0]
    return jnp.where(index == lax.broadcasted_iota(jnp.int32, (slots, width), 1), 1.0, 0.0)


def halves_side_by_side(tile):
    half = tile.shape[0] // 2
    return jnp.concatenate([tile[:half], tile[half:]], axis=1)


def pack_rows(row_ref, col_ref, h_ref, piece_ref, rows_ref):
    width = h_ref.shape[1]
    rows = across(one_hot(row_ref[...], h_ref.shape[0]), h_ref[...], ((1,), (0,)), HIGH)
    piece = across(rows, one_hot(col_ref[...], width), ((1,), (1,)), HIGH)
    piece = halves_side_by_side(piece)
    half = rows.shape[0] // 2
    for d in range(piece_ref.shape[0]):
        piece_ref[d] = piece
        rows_ref[d] = rows[half * (d % 2) : half * (d % 2) + half]


def pack_cols(col_ref, h_ref, w_ref, out_ref):
    pick = one_hot(col_ref[...], h_ref.shape[1])
    w = across(pick.astype(BF16), w_ref[...], ((1,), (1,))).astype(BF16)
    c = across(pick, h_ref[...], ((1,), (1,)), HIGH)
    c_high = c.astype(BF16)
    c_low = (c - c_high.astype(F32)).astype(BF16)
    packed = jnp.concatenate([w, c_high, c_low], axis=1)
    for d in range(out_ref.shape[0]):
        out_ref[d] = packed


def pack_slab(first_ref, core_ref, got_ref, out_ref, slab_ref):
    tiles, half, both = got_ref.shape
    cap = both // 2
    for t in range(tiles):
        slab_ref[pl.ds(first_ref[t], half), 0:cap] = got_ref[t, :, 0:cap]
        slab_ref[pl.ds(first_ref[t] + half, half), 0:cap] = got_ref[t, :, cap:both]
    span = out_ref.shape[2]
    mine = slab_ref[pl.ds(pl.multiple_of(core_ref[0] * span, span), span), :]
    mine = mine.T[0:cap, :]
    for d in range(tiles):
        out_ref[d] = mine


def place_rows(ref, at, start, value):
    rows, width = value.shape
    for j in range(0, width, 128):
        strip = value[:, j : j + 128]
        ref[at + j // 128, pl.ds(start, rows), 0 : strip.shape[1]] = strip


def rows_at(ref, start, rows, width):
    strips = [ref[j, pl.ds(start, rows), :] for j in range(ref.shape[0])]
    return jnp.concatenate(strips, axis=1)[:, :width]


def spread(v, i):
    return jnp.broadcast_to(v[i : i + 1, :], v.shape)


def invert_base(tiles):
    width = tiles[0].shape[1]
    lane = lax.broadcasted_iota(jnp.int32, (8, width), 1)
    sub = lax.broadcasted_iota(jnp.int32, (8, width), 0)
    tiles = list(tiles)
    count = len(tiles)
    for t in range(count):
        q = 8 * t
        own = tiles[t]
        cols = [jnp.broadcast_to(own[:, q + j : q + j + 1], (8, width)) for j in range(8)]
        here = (lane >= q) & (lane < q + 8)
        panel = jnp.where(here, jnp.where(lane - q == sub, 1.0, 0.0), own)
        for j in range(0, 8, 2):
            k = j + 1
            a, b, b2, c = spread(cols[j], j), spread(cols[k], j), spread(cols[j], k), spread(cols[k], k)
            r = 1.0 / (a * c - b * b2)
            i00, i01, i10, i11 = c * r, -(b * r), -(b2 * r), a * r
            is_j, is_k = sub == j, sub == k
            f_j = jnp.where(is_j, -i00, jnp.where(is_k, -i10, cols[j] * i00 + cols[k] * i10))
            f_k = jnp.where(is_j, -i01, jnp.where(is_k, -i11, cols[j] * i01 + cols[k] * i11))
            pivot = is_j | is_k

            def swept(v):
                return jnp.where(pivot, 0.0, v) - (f_j * spread(v, j) + f_k * spread(v, k))

            for m in range(j + 2, 8):
                cols[m] = swept(cols[m])
            panel = swept(panel)
        rows = [spread(panel, j) for j in range(8)]
        for s in range(1, count):
            s = (t + s) % count
            v = tiles[s]
            p = [jnp.broadcast_to(v[:, q + j : q + j + 1], (8, width)) * rows[j] for j in range(8)]
            total = ((p[0] + p[1]) + (p[2] + p[3])) + ((p[4] + p[5]) + (p[6] + p[7]))
            tiles[s] = jnp.where(here, 0.0, v) - total
        tiles[t] = panel
    return tiles


def invert(first_ref, core_ref, own_ref, other_ref, out_ref, block_ref):
    tiles, cap, span = own_ref.shape
    low_is_own = core_ref[0] == 0
    n = out_ref.shape[0]
    for t in range(tiles):
        own, other = own_ref[t], other_ref[t]
        place_rows(block_ref, 0, first_ref[t], jnp.where(low_is_own, own, other))
        place_rows(block_ref, span // 128, first_ref[t], jnp.where(low_is_own, other, own))
    for j in range(n // 128):
        out_ref[:, 128 * j : 128 * j + 128] = block_ref[j, 0:n, :]
    for lo in range(0, n, BASE):
        hi = lo + BASE
        diagonal = out_ref[lo:hi, lo:hi]
        base = jnp.concatenate(invert_base([diagonal[s : s + 8] for s in range(0, BASE, 8)]), axis=0)
        cols = out_ref[:, lo:hi]
        rows = jnp.dot(base, out_ref[lo:hi, :], precision=HIGH, preferred_element_type=F32)
        rows = jnp.concatenate([p for p in (rows[:, :lo], base, rows[:, hi:]) if p.shape[1]], axis=1)
        lane = lax.broadcasted_iota(jnp.int32, (BASE, n), 1)
        here = (lane >= lo) & (lane < hi)
        for r in range(0, n, BASE):
            if r != lo:
                kept = jnp.where(here, 0.0, out_ref[r : r + BASE, :])
                out_ref[r : r + BASE, :] = kept - jnp.dot(
                    cols[r : r + BASE], rows, precision=HIGH, preferred_element_type=F32
                )
        out_ref[lo:hi, :] = rows


def update(first_ref, count_ref, core_ref, col_ref, inv_ref, own_ref, other_ref, got_ref, h_ref, w_ref,
           h_out_ref, w_out_ref, panel_ref, high_ref, low_ref):
    step = pl.program_id(0)
    tiles, half, width = own_ref.shape
    cap = 2 * half
    n = inv_ref.shape[0]
    block = w_ref.shape[0]
    rows_w = block * pl.num_programs(0)

    @pl.when(step == 0)
    def _():
        low_is_own = core_ref[0] == 0
        for t in range(tiles):
            own, other = own_ref[t], other_ref[t]
            place_rows(panel_ref, 0, first_ref[t], jnp.where(low_is_own, own, other))
            place_rows(panel_ref, 0, first_ref[t] + half, jnp.where(low_is_own, other, own))
        panel = rows_at(panel_ref, 0, n, width)
        solved = jnp.dot(inv_ref[...], panel, precision=HIGH, preferred_element_type=F32)
        place_rows(panel_ref, 0, 0, solved)
        slot = lax.broadcasted_iota(jnp.int32, (cap, width), 0)
        for t in range(tiles):
            s = jnp.where(slot < count_ref[t], rows_at(panel_ref, first_ref[t], cap, width), 0.0)
            s_high = s.astype(BF16)
            high_ref[t * cap : (t + 1) * cap, :] = s_high
            low_ref[t * cap : (t + 1) * cap, :] = (s - s_high.astype(F32)).astype(BF16)
        at = rows_w
        c_high = got_ref[:, :, at : at + width].reshape(tiles * cap, width)
        c_low = got_ref[:, :, at + width : at + 2 * width].reshape(tiles * cap, width)
        both = ((0,), (0,))
        total = across(c_high, high_ref[...], both)
        total = total + (across(c_high, low_ref[...], both) + across(c_low, high_ref[...], both))
        h_out_ref[...] = h_ref[...] - total

    keep = 1.0 - jnp.sum(one_hot(col_ref[...], width), axis=0, keepdims=True)
    cols = got_ref[:, :, pl.ds(pl.multiple_of(step * block, block), block)].reshape(tiles * cap, block)
    total = across(cols, high_ref[...], ((0,), (0,))) + across(cols, low_ref[...], ((0,), (0,)))
    w_out_ref[...] = (w_ref[...].astype(F32) - total) * keep


def sent_to_all(copies, axis):
    return lax.all_to_all(copies, axis, split_axis=0, concat_axis=0, tiled=True)


def on_device(hessian_inverse, weights, pruned):
    tile_rows, tile_cols = hessian_inverse.shape
    rows_w = weights.shape[0]
    n = pruned.shape[0]
    tiles = lax.axis_size("row")
    cap = 2 * n // tiles
    half = cap // 2
    row, col = lax.axis_index("row"), lax.axis_index("col")
    core = (row % 2).astype(jnp.int32).reshape(1)
    edges = jnp.arange(tiles + 1, dtype=jnp.int32) * tile_cols
    ends = jnp.sum((pruned[None, :] < edges[:, None]).astype(jnp.int32), axis=1)
    first, count = ends[:-1], ends[1:] - ends[:-1]

    def slots(tile):
        got = lax.dynamic_slice(jnp.pad(pruned, (0, cap)), (first[tile],), (cap,))
        got = jnp.where(jnp.arange(cap) < count[tile], got - tile * tile_cols, -1)
        return got.reshape(cap, 1)

    row_index, col_index = slots(row), slots(col)
    pieces, rows = pl.pallas_call(
        pack_rows,
        out_shape=(
            jax.ShapeDtypeStruct((tiles, half, 2 * cap), F32),
            jax.ShapeDtypeStruct((tiles, half, tile_cols), F32),
        ),
        in_specs=[VMEM] * 3,
        out_specs=(VMEM, VMEM),
        name="pack_rows",
    )(row_index, col_index, hessian_inverse)
    pieces = sent_to_all(pieces, "row")
    packed = pl.pallas_call(
        pack_cols,
        out_shape=jax.ShapeDtypeStruct((tiles, cap, rows_w + 2 * tile_rows), BF16),
        in_specs=[VMEM] * 3,
        out_specs=VMEM,
        name="pack_cols",
    )(col_index, hessian_inverse, weights)
    packed = sent_to_all(packed, "col")
    slab = pl.pallas_call(
        pack_slab,
        out_shape=jax.ShapeDtypeStruct((tiles, cap, n // 2), F32),
        in_specs=[SMEM, SMEM, VMEM],
        out_specs=VMEM,
        scratch_shapes=[pltpu.VMEM((n + cap, 2 * cap), F32)],
        name="pack_slab",
    )(first, core, pieces)
    slab = sent_to_all(slab, "col")
    rows = sent_to_all(rows, "row")
    twin = [(i, i ^ 1) for i in range(tiles)]
    slab_twin = lax.ppermute(slab, "row", twin)
    inverse = pl.pallas_call(
        invert,
        out_shape=jax.ShapeDtypeStruct((n, n), F32),
        in_specs=[SMEM, SMEM, VMEM, VMEM],
        out_specs=VMEM,
        scratch_shapes=[pltpu.VMEM((n // 128, n + cap, 128), F32)],
        name="invert",
    )(first, core, slab, slab_twin)
    rows_twin = lax.ppermute(rows, "row", twin)
    block = rows_w // 8
    whole = lambda shape: pl.BlockSpec(shape, lambda i: (0,) * len(shape), pipeline_mode=pl.Buffered(1))
    return pl.pallas_call(
        update,
        grid=(8,),
        out_shape=(
            jax.ShapeDtypeStruct(hessian_inverse.shape, F32),
            jax.ShapeDtypeStruct(weights.shape, F32),
        ),
        in_specs=[SMEM, SMEM, SMEM]
        + [whole(a.shape) for a in (col_index, inverse, rows, rows_twin, packed, hessian_inverse)]
        + [pl.BlockSpec((block, tile_cols), lambda i: (i, 0))],
        out_specs=(
            whole(hessian_inverse.shape),
            pl.BlockSpec((block, tile_cols), lambda i: (i, 0)),
        ),
        scratch_shapes=[
            pltpu.VMEM((-(-tile_cols // 128), n + cap, 128), F32),
            pltpu.VMEM((tiles * cap, tile_cols), BF16),
            pltpu.VMEM((tiles * cap, tile_cols), BF16),
        ],
        name="update",
    )(first, count, core, col_index, inverse, rows, rows_twin, packed, hessian_inverse, weights)


def solution(mesh):
    specs = (P("row", "col"), P("row", "col"))
    return jax.shard_map(on_device, mesh=mesh, in_specs=(*specs, P()), out_specs=specs, check_vma=False)
```

```python
import functools
import math

import jax
import jax.numpy as jnp
from jax import lax
from jax.experimental import pallas as pl
from jax.experimental.pallas import tpu as pltpu
from jax.sharding import PartitionSpec as P


HIGH = lax.Precision.HIGHEST
F32 = jnp.float32
BF16 = jnp.bfloat16
VMEM = pl.BlockSpec(memory_space=pltpu.VMEM)
SMEM = pl.BlockSpec(memory_space=pltpu.SMEM)
BASE = 128


def across(a, b, dims, precision=None):
    return lax.dot_general(a, b, (dims, ((), ())), precision=precision, preferred_element_type=F32)


def one_hot(index, width):
    slots = index.shape[0]
    return jnp.where(index == lax.broadcasted_iota(jnp.int32, (slots, width), 1), 1.0, 0.0)


def held(pruned, tile, width, place):
    low = tile * width
    before = jnp.sum(jnp.where(pruned < low, 1, 0), axis=1, keepdims=True)
    place = place(before)
    lane = lax.broadcasted_iota(jnp.int32, (place.shape[0], pruned.shape[1]), 1)
    here = (lane == place) & (pruned >= low) & (pruned < low + width)
    return jnp.sum(jnp.where(here, pruned - low + 1, 0), axis=1, keepdims=True) - 1


def in_turn(cap):
    slot = lax.broadcasted_iota(jnp.int32, (cap, 1), 0)
    return lambda before: before + slot


def dealt(cap, hands):
    slot = lax.broadcasted_iota(jnp.int32, (cap, 1), 0)
    each = cap // hands
    hand, turn = slot // each, slot % each

    def place(before):
        return hand + hands * ((before - hand + hands - 1) // hands + turn)

    return place


def pack_rows(at_ref, pruned_ref, h_ref, rows_ref):
    height, _ = h_ref.shape
    pruned = pruned_ref[...]
    tiles = rows_ref.shape[0]
    cap = 2 * pruned.shape[1] // tiles
    pick = one_hot(held(pruned, at_ref[0], height, in_turn(cap)), height)
    rows = across(pick, h_ref[...], ((1,), (0,)), HIGH)
    for core in range(2):
        part = strips_of(rows[cap // 2 * core : cap // 2 * (core + 1)])
        for d in range(core, tiles, 2):
            rows_ref[d] = part


def strips_of(rows):
    count, width = rows.shape
    full = width // 128 * 128
    rest = width - full
    groups = 128 // rest
    each = count // groups
    strips = [rows[:, j : j + 128] for j in range(0, full, 128)]
    strips.append(jnp.concatenate([rows[each * i : each * i + each, full:] for i in range(groups)], axis=1))
    return jnp.concatenate(strips, axis=0)


def place_strips(ref, start, packed, count, width):
    full = width // 128
    rest = width - 128 * full
    each = count * rest // 128
    for j in range(full):
        ref[j, pl.ds(start, count), :] = packed[count * j : count * j + count]
    last = packed[count * full :]
    for i in range(128 // rest):
        ref[full, pl.ds(start + each * i, each), 0:rest] = last[:, rest * i : rest * i + rest]


def pack_cols(at_ref, pruned_ref, h_ref, w_ref, out_ref):
    pruned = pruned_ref[...]
    cap = out_ref.shape[0]
    width = h_ref.shape[1]
    tiles = 2 * pruned.shape[1] // cap
    pick = one_hot(held(pruned, at_ref[1], width, dealt(cap, tiles)), width)
    w = across(pick.astype(BF16), w_ref[...], ((1,), (0,))).astype(BF16)
    c = across(pick, h_ref[...], ((1,), (1,)), HIGH)
    c_high = c.astype(BF16)
    c_low = (c - c_high.astype(F32)).astype(BF16)
    out_ref[...] = jnp.concatenate([w, c_high, c_low], axis=1)


def gather_hand(at_ref, pruned_ref, got_ref, low_ref, high_ref, piece_ref, *, height, width):
    pruned = pruned_ref[...]
    cap, length = got_ref.shape
    tiles = piece_ref.shape[0]
    mine = cap // 2
    each = cap // tiles
    slot = lax.broadcasted_iota(jnp.int32, (cap, 1), 0)
    tile, turn = slot // each, slot % each
    before = jnp.sum(jnp.where(pruned < tile * width, 1, 0), axis=1, keepdims=True)
    after = jnp.sum(jnp.where(pruned < tile * width + width, 1, 0), axis=1, keepdims=True)
    hand = at_ref[1]
    turn = (before - hand + tiles - 1) // tiles + turn
    place = hand + tiles * turn
    turn = jnp.where(place < after, turn, -1)
    out = across(one_hot(turn, mine).astype(BF16), got_ref[...], ((0,), (0,)))
    cols = out[:, length - 2 * height : length - height] + out[:, length - height :]
    pick = one_hot(held(pruned, at_ref[0], height, in_turn(cap)), height)
    piece = across(pick, cols, ((1,), (1,)), HIGH)
    quarter = cap // 4
    piece = jnp.concatenate([piece[quarter * i : quarter * i + quarter] for i in range(4)], axis=1)
    for d in range(tiles):
        piece_ref[d] = piece
    low_ref[...] = out[: mine // 2].astype(BF16)
    high_ref[...] = out[mine // 2 :].astype(BF16)


def pack_slab(first_ref, at_ref, got_ref, out_ref, slab_ref, turned_ref):
    tiles, quarter, four = got_ref.shape
    mine = four // 4
    for t in range(tiles):
        got = got_ref[t]
        for i in range(4):
            slab_ref[pl.ds(first_ref[t] + quarter * i, quarter), 0:mine] = got[:, mine * i : mine * i + mine]
    turned_ref[...] = slab_ref[0 : turned_ref.shape[1], :].T[0:mine, :]
    half = mine // 2
    slab = turned_ref[pl.ds(pl.multiple_of(at_ref[0] % 2 * half, half), half), :]
    for d in range(tiles):
        out_ref[d] = slab


def place_rows(ref, at, start, value):
    rows, width = value.shape
    for j in range(0, width, 128):
        strip = value[:, j : j + 128]
        ref[at + j // 128, pl.ds(start, rows), 0 : strip.shape[1]] = strip


def rows_at(ref, start, rows, width):
    strips = [ref[j, pl.ds(start, rows), :] for j in range(ref.shape[0])]
    return jnp.concatenate(strips, axis=1)[:, :width]


def spread(v, i):
    return jnp.broadcast_to(v[i : i + 1, :], v.shape)


def invert_base(tiles):
    width = tiles[0].shape[1]
    lane = lax.broadcasted_iota(jnp.int32, (8, width), 1)
    sub = lax.broadcasted_iota(jnp.int32, (8, width), 0)
    tiles = list(tiles)
    count = len(tiles)
    for t in range(count):
        q = 8 * t
        own = tiles[t]
        cols = [jnp.broadcast_to(own[:, q + j : q + j + 1], (8, width)) for j in range(8)]
        here = (lane >= q) & (lane < q + 8)
        panel = jnp.where(here, jnp.where(lane - q == sub, 1.0, 0.0), own)
        for j in range(0, 8, 2):
            k = j + 1
            a, b, b2, c = spread(cols[j], j), spread(cols[k], j), spread(cols[j], k), spread(cols[k], k)
            r = 1.0 / (a * c - b * b2)
            i00, i01, i10, i11 = c * r, -(b * r), -(b2 * r), a * r
            is_j, is_k = sub == j, sub == k
            f_j = jnp.where(is_j, -i00, jnp.where(is_k, -i10, cols[j] * i00 + cols[k] * i10))
            f_k = jnp.where(is_j, -i01, jnp.where(is_k, -i11, cols[j] * i01 + cols[k] * i11))
            pivot = is_j | is_k

            def swept(v):
                return jnp.where(pivot, 0.0, v) - (f_j * spread(v, j) + f_k * spread(v, k))

            for m in range(j + 2, 8):
                cols[m] = swept(cols[m])
            panel = swept(panel)
        rows = [spread(panel, j) for j in range(8)]
        for s in range(1, count):
            s = (t + s) % count
            v = tiles[s]
            p = [jnp.broadcast_to(v[:, q + j : q + j + 1], (8, width)) * rows[j] for j in range(8)]
            total = ((p[0] + p[1]) + (p[2] + p[3])) + ((p[4] + p[5]) + (p[6] + p[7]))
            tiles[s] = jnp.where(here, 0.0, v) - total
        tiles[t] = panel
    return tiles


def invert(at_ref, own_ref, other_ref, out_ref, block_ref):
    tiles, half, n = own_ref.shape
    low_is_own = at_ref[0] % 2 == 0
    for t in range(tiles):
        own, other = own_ref[t], other_ref[t]
        low, high = jnp.where(low_is_own, own, other), jnp.where(low_is_own, other, own)
        for j in range(n // 128):
            lanes = slice(128 * j, 128 * j + 128)
            block_ref[j, pl.ds(t, half, stride=tiles), :] = low[:, lanes]
            block_ref[j, pl.ds(t + half * tiles, half, stride=tiles), :] = high[:, lanes]
    for j in range(n // 128):
        out_ref[:, 128 * j : 128 * j + 128] = block_ref[j]
    for lo in range(0, n, BASE):
        hi = lo + BASE
        diagonal = out_ref[lo:hi, lo:hi]
        base = jnp.concatenate(invert_base([diagonal[s : s + 8] for s in range(0, BASE, 8)]), axis=0)
        cols = out_ref[:, lo:hi]
        rows = jnp.dot(base, out_ref[lo:hi, :], precision=HIGH, preferred_element_type=F32)
        rows = jnp.concatenate([p for p in (rows[:, :lo], base, rows[:, hi:]) if p.shape[1]], axis=1)
        lane = lax.broadcasted_iota(jnp.int32, (BASE, n), 1)
        here = (lane >= lo) & (lane < hi)
        for r in range(0, n, BASE):
            if r != lo:
                kept = jnp.where(here, 0.0, out_ref[r : r + BASE, :])
                out_ref[r : r + BASE, :] = kept - jnp.dot(
                    cols[r : r + BASE], rows, precision=HIGH, preferred_element_type=F32
                )
        out_ref[lo:hi, :] = rows


def update(first_ref, at_ref, pruned_ref, inv_ref, own_ref, other_ref, *refs):
    blocks, (h_ref, w_ref, h_out_ref, w_out_ref, panel_ref, high_ref, low_ref, keep_ref) = refs[:-8], refs[-8:]
    step = pl.program_id(0)
    tiles = own_ref.shape[0]
    n = inv_ref.shape[0]
    width = h_ref.shape[1]
    half = n // tiles
    side = len(blocks) // 2
    block = w_ref.shape[1]
    rows_w = block * pl.num_programs(0)
    apply = ((1,), (0,))

    def cols(start, size):
        return jnp.concatenate([b[:, pl.ds(start, size)] for b in blocks], axis=0)

    @pl.when(step == 0)
    def _():
        low_is_own = at_ref[0] % 2 == 0
        for t in range(tiles):
            own, other = own_ref[t], other_ref[t]
            place_strips(panel_ref, first_ref[t], jnp.where(low_is_own, own, other), half, width)
            place_strips(panel_ref, first_ref[t] + half, jnp.where(low_is_own, other, own), half, width)
        panel = rows_at(panel_ref, 0, n, width)
        solved = jnp.dot(inv_ref[...], panel, precision=HIGH, preferred_element_type=F32)
        place_rows(panel_ref, 0, 0, solved)
        x, y = at_ref[1] % side, at_ref[1] // side
        hands = []
        for path in range(2):
            for far in range(side):
                for near in range(side):
                    dx, dy = (near, far) if path == 0 else (far, near)
                    hand = (y + side - dy) % side * side + (x + side - dx) % side
                    hands.append(hand + path * (n // 2))
        solved = jnp.concatenate(
            [
                jnp.concatenate([panel_ref[j, pl.ds(h, n // tiles // 2, stride=tiles), :] for h in hands], axis=0)
                for j in range(panel_ref.shape[0])
            ],
            axis=1,
        ).T[:width, :]
        high = solved.astype(BF16)
        high_ref[...] = high
        low_ref[...] = (solved - high.astype(F32)).astype(BF16)
        c_high, c_low = cols(rows_w, width), cols(rows_w + width, width)
        total = across(high_ref[...], c_high, apply)
        total = total + (across(low_ref[...], c_high, apply) + across(high_ref[...], c_low, apply))
        h_out_ref[...] = h_ref[...] - total.T
        unit = lax.broadcasted_iota(jnp.int32, (width, n), 0) + at_ref[1] * width
        hits = jnp.sum(jnp.where(unit == pruned_ref[...], 1.0, 0.0), axis=1, keepdims=True)
        keep_ref[...] = jnp.broadcast_to(1.0 - hits, keep_ref.shape)

    got = cols(pl.multiple_of(step * block, block), block)
    total = across(high_ref[...], got, apply) + across(low_ref[...], got, apply)
    w_out_ref[...] = (w_ref[...].astype(F32) - total) * keep_ref[:, 0:1]


def sent_to_all(copies, axis):
    return lax.all_to_all(copies, axis, split_axis=0, concat_axis=0, tiled=True)


def on_device(hessian_inverse, weights, pruned):
    tile_rows, tile_cols = hessian_inverse.shape
    rows_w = weights.shape[0]
    n = pruned.shape[0]
    tiles = lax.axis_size("row")
    cap = 2 * n // tiles
    half = cap // 2
    at = jnp.stack([lax.axis_index("row"), lax.axis_index("col")]).astype(jnp.int32)
    weights = weights.T
    listed = pruned.reshape(1, n)
    edges = jnp.arange(tiles, dtype=jnp.int32) * tile_cols
    first = jnp.sum((listed < edges[:, None]).astype(jnp.int32), axis=1)
    length = rows_w + 2 * tile_rows
    hands = pl.pallas_call(
        pack_cols,
        out_shape=jax.ShapeDtypeStruct((cap, length), BF16),
        in_specs=[SMEM, VMEM, VMEM, VMEM],
        out_specs=VMEM,
        name="pack_cols",
    )(at, listed, hessian_inverse, weights)
    hands = sent_to_all(hands, "col")
    mine = n // tiles
    rows = pl.pallas_call(
        pack_rows,
        out_shape=jax.ShapeDtypeStruct((tiles, half * tile_cols // 128, 128), F32),
        in_specs=[SMEM, VMEM, VMEM],
        out_specs=VMEM,
        name="pack_rows",
    )(at, listed, hessian_inverse)
    low, high, pieces = pl.pallas_call(
        functools.partial(gather_hand, height=tile_rows, width=tile_cols),
        out_shape=(
            jax.ShapeDtypeStruct((mine // 2, length), BF16),
            jax.ShapeDtypeStruct((mine // 2, length), BF16),
            jax.ShapeDtypeStruct((tiles, cap // 4, 4 * mine), F32),
        ),
        in_specs=[SMEM, VMEM, VMEM],
        out_specs=(VMEM, VMEM, VMEM),
        name="gather_hand",
    )(at, listed, hands)
    pieces = sent_to_all(pieces, "row")
    side = math.isqrt(tiles)

    def along_x(value, d):
        return lax.ppermute(value, "col", [(c, c // side * side + (c + d) % side) for c in range(tiles)])

    def along_y(value, d):
        return lax.ppermute(value, "col", [(c, (c + d * side) % tiles) for c in range(tiles)])

    low = jnp.concatenate([low] + [along_x(low, d) for d in range(1, side)], axis=0)
    high = jnp.concatenate([high] + [along_y(high, d) for d in range(1, side)], axis=0)
    slab = pl.pallas_call(
        pack_slab,
        out_shape=jax.ShapeDtypeStruct((tiles, mine // 2, n), F32),
        in_specs=[SMEM, SMEM, VMEM],
        out_specs=VMEM,
        scratch_shapes=[pltpu.VMEM((n + cap, 128), F32), pltpu.VMEM((mine, n), F32)],
        name="pack_slab",
    )(first, at, pieces)
    slab = sent_to_all(slab, "col")
    cols = [low] + [along_y(low, d) for d in range(1, side)]
    cols += [high] + [along_x(high, d) for d in range(1, side)]
    rows = sent_to_all(rows, "row")
    twin = [(i, i ^ 1) for i in range(tiles)]
    slab_twin = lax.ppermute(slab, "row", twin)
    inverse = pl.pallas_call(
        invert,
        out_shape=jax.ShapeDtypeStruct((n, n), F32),
        in_specs=[SMEM, VMEM, VMEM],
        out_specs=VMEM,
        scratch_shapes=[pltpu.VMEM((n // 128, n, 128), F32)],
        name="invert",
    )(at, slab, slab_twin)
    rows_twin = lax.ppermute(rows, "row", twin)
    steps = 8
    block = rows_w // steps
    whole = lambda shape: pl.BlockSpec(shape, lambda i: (0,) * len(shape), pipeline_mode=pl.Buffered(1))
    strip = pl.BlockSpec((tile_cols, block), lambda i: (0, i))
    h_new, w_new = pl.pallas_call(
        update,
        grid=(steps,),
        out_shape=(
            jax.ShapeDtypeStruct(hessian_inverse.shape, F32),
            jax.ShapeDtypeStruct(weights.shape, F32),
        ),
        in_specs=[SMEM, SMEM] + [whole(a.shape) for a in (listed, inverse, rows, rows_twin, *cols, hessian_inverse)] + [strip],
        out_specs=(whole(hessian_inverse.shape), strip),
        scratch_shapes=[
            pltpu.VMEM((-(-tile_cols // 128), n + cap, 128), F32),
            pltpu.VMEM((tile_cols, n), BF16),
            pltpu.VMEM((tile_cols, n), BF16),
            pltpu.VMEM((tile_cols, 128), F32),
        ],
        name="update",
    )(first, at, listed, inverse, rows, rows_twin, *cols, hessian_inverse, weights)
    return h_new, w_new.T


def solution(mesh):
    specs = (P("row", "col"), P("row", "col"))

    return jax.shard_map(on_device, mesh=mesh, in_specs=(*specs, P()), out_specs=specs, check_vma=False)
```

```python
import functools
import math

import jax
import jax.numpy as jnp
from jax import lax
from jax.experimental import pallas as pl
from jax.experimental.pallas import tpu as pltpu
from jax.sharding import PartitionSpec as P


HIGH = lax.Precision.HIGHEST
F32 = jnp.float32
BF16 = jnp.bfloat16
VMEM = pl.BlockSpec(memory_space=pltpu.VMEM)
SMEM = pl.BlockSpec(memory_space=pltpu.SMEM)
BASE = 128


def across(a, b, dims, precision=None):
    return lax.dot_general(a, b, (dims, ((), ())), precision=precision, preferred_element_type=F32)


def one_hot(index, width):
    slots = index.shape[0]
    return jnp.where(index == lax.broadcasted_iota(jnp.int32, (slots, width), 1), 1.0, 0.0)


def held(pruned, tile, width, place):
    low = tile * width
    before = jnp.sum(jnp.where(pruned < low, 1, 0), axis=1, keepdims=True)
    place = place(before)
    lane = lax.broadcasted_iota(jnp.int32, (place.shape[0], pruned.shape[1]), 1)
    here = (lane == place) & (pruned >= low) & (pruned < low + width)
    return jnp.sum(jnp.where(here, pruned - low + 1, 0), axis=1, keepdims=True) - 1


def in_turn(cap):
    slot = lax.broadcasted_iota(jnp.int32, (cap, 1), 0)
    return lambda before: before + slot


def dealt(before, tiles, slots):
    slot = lax.broadcasted_iota(jnp.int32, (tiles * 2 * slots, 1), 0)
    hand, second, turn = slot // (2 * slots), slot // slots % 2, slot % slots
    return hand, second, (before - hand + tiles - 1) // tiles + turn


def lanes_for(width):
    return -(-width // 128) * 128


def pack_rows(at_ref, pruned_ref, h_ref, mine_ref, other_ref):
    height = h_ref.shape[0]
    pick = one_hot(held(pruned_ref[...], at_ref[0], height, in_turn(2 * mine_ref.shape[0] * 128 // h_ref.shape[1])), height)
    rows = across(pick, h_ref[...], ((1,), (0,)), HIGH)
    half = rows.shape[0] // 2
    low, high = strips_of(rows[:half]), strips_of(rows[half:])
    core = at_ref[0] % 2
    mine_ref[...] = jnp.where(core == 0, low, high)
    other_ref[...] = jnp.where(core == 0, high, low)


def strips_of(rows):
    count, width = rows.shape
    full = width // 128 * 128
    rest = width - full
    groups = 128 // rest
    each = count // groups
    strips = [rows[:, j : j + 128] for j in range(0, full, 128)]
    strips.append(jnp.concatenate([rows[each * i : each * i + each, full:] for i in range(groups)], axis=1))
    return jnp.concatenate(strips, axis=0)


def place_strips(ref, start, packed, count, width):
    full = width // 128
    rest = width - 128 * full
    each = count * rest // 128
    for j in range(full):
        ref[j, pl.ds(start, count), :] = packed[count * j : count * j + count]
    last = packed[count * full :]
    for i in range(128 // rest):
        ref[full, pl.ds(start + each * i, each), 0:rest] = last[:, rest * i : rest * i + rest]


def pack_cols(at_ref, pruned_ref, h_ref, w_ref, out_ref):
    pruned = pruned_ref[...]
    slots, half = out_ref.shape
    width = h_ref.shape[1]
    tiles = slots // 8
    pick = one_hot(held(pruned, at_ref[1], width, lambda before: dealt_places(before, tiles, 4)), width)
    w = w_ref[...]
    picked = pick.astype(BF16)
    first = across(picked, w[:, :half], ((1,), (0,)))
    last = across(picked, w[:, half:], ((1,), (0,)))
    c = across(pick, h_ref[...], ((1,), (1,)), HIGH)
    c_high = c.astype(BF16).astype(F32)
    spare = jnp.zeros((slots, lanes_for(width) - width), F32)
    last = jnp.concatenate([last, c_high, spare, c - c_high, spare], axis=1)
    second = lax.broadcasted_iota(jnp.int32, (slots, 1), 0) // 4 % 2
    out_ref[...] = jnp.where(second == 1, last, first).astype(BF16)


def dealt_places(before, tiles, slots):
    hand, _, turn = dealt(before, tiles, slots)
    return hand + tiles * turn


def gather_hand(at_ref, pruned_ref, got_ref, low_ref, high_ref, piece_ref, *, height, width):
    pruned = pruned_ref[...]
    slots, half = got_ref.shape
    tiles = piece_ref.shape[0]
    mine = pruned.shape[1] // tiles
    slot = lax.broadcasted_iota(jnp.int32, (slots, 1), 0)
    tile, second, turn = slot // 8, slot // 4 % 2, slot % 4
    before = jnp.sum(jnp.where(pruned < tile * width, 1, 0), axis=1, keepdims=True)
    after = jnp.sum(jnp.where(pruned < tile * width + width, 1, 0), axis=1, keepdims=True)
    hand = at_ref[1]
    turn = (before - hand + tiles - 1) // tiles + turn
    turn = jnp.where(hand + tiles * turn < after, turn, -1)
    got = got_ref[...]
    parts = [
        across(one_hot(jnp.where(second == part, turn, -1), mine).astype(BF16), got, ((0,), (0,)))
        for part in range(2)
    ]
    wide = lanes_for(height)
    c = parts[1][:, half - 2 * wide : half - 2 * wide + height] + parts[1][:, half - wide : half - wide + height]
    cap = 2 * mine
    pick = one_hot(held(pruned, at_ref[0], height, in_turn(cap)), height)
    piece = across(pick, c, ((1,), (1,)), HIGH)
    quarter = cap // 4
    piece = jnp.concatenate([piece[quarter * i : quarter * i + quarter] for i in range(4)], axis=1)
    for d in range(tiles):
        piece_ref[d] = piece
    for part in range(2):
        lanes = slice(half * part, half * part + half)
        low_ref[:, lanes] = parts[part][: mine // 2].astype(BF16)
        high_ref[:, lanes] = parts[part][mine // 2 :].astype(BF16)


def join(*refs):
    count = (len(refs) - 2) // 2
    for path in range(2):
        out = refs[2 * count + path]
        rows = out.shape[0] // count
        for d in range(count):
            out[rows * d : rows * d + rows, :] = refs[count * path + d][...]


def pack_slab(first_ref, at_ref, got_ref, out_ref, slab_ref, turned_ref):
    tiles, quarter, four = got_ref.shape
    mine = four // 4
    for t in range(tiles):
        got = got_ref[t]
        for i in range(4):
            slab_ref[pl.ds(first_ref[t] + quarter * i, quarter), 0:mine] = got[:, mine * i : mine * i + mine]
    turned_ref[...] = slab_ref[0 : turned_ref.shape[1], :].T[0:mine, :]
    half = mine // 2
    slab = turned_ref[pl.ds(pl.multiple_of(at_ref[0] % 2 * half, half), half), :]
    for d in range(tiles):
        out_ref[d] = slab


def place_rows(ref, at, start, value):
    rows, width = value.shape
    for j in range(0, width, 128):
        strip = value[:, j : j + 128]
        ref[at + j // 128, pl.ds(start, rows), 0 : strip.shape[1]] = strip


def rows_at(ref, start, rows, width):
    strips = [ref[j, pl.ds(start, rows), :] for j in range(ref.shape[0])]
    return jnp.concatenate(strips, axis=1)[:, :width]


def spread(v, i):
    return jnp.broadcast_to(v[i : i + 1, :], v.shape)


def base_factors(tiles, zero, work):
    width = tiles[0].shape[1]
    lane = lax.broadcasted_iota(jnp.int32, (8, width), 1)
    sub = lax.broadcasted_iota(jnp.int32, (8, width), 0)
    tiles = list(tiles)
    count = len(tiles)
    lower, scaled = [], []
    for t in range(count):
        q = 8 * t
        own = tiles[t]
        cols = [jnp.broadcast_to(own[:, q + j : q + j + 1], (8, width)) + zero for j in range(8)]
        here = (lane >= q) & (lane < q + 8)
        known = lane < q + 8
        panel = jnp.where(here, jnp.where(lane - q == sub, 1.0, 0.0), own)
        lower.append(jnp.where(known, panel, 0.0))
        for j in range(0, 8, 2):
            k = j + 1
            a, b, b2, c = spread(cols[j], j), spread(cols[k], j), spread(cols[j], k), spread(cols[k], k)
            r = 1.0 / (a * c - b * b2)
            i00, i01, i10, i11 = c * r, -(b * r), -(b2 * r), a * r
            is_j, is_k = sub == j, sub == k
            f_j = jnp.where(is_j, -i00, jnp.where(is_k, -i10, cols[j] * i00 + cols[k] * i10))
            f_k = jnp.where(is_j, -i01, jnp.where(is_k, -i11, cols[j] * i01 + cols[k] * i11))
            pivot = is_j | is_k

            def swept(v):
                return jnp.where(pivot, 0.0, v) - (f_j * spread(v, j) + f_k * spread(v, k))

            for m in range(j + 2, 8):
                cols[m] = swept(cols[m])
            panel = swept(panel)
        scaled.append(jnp.where(known, panel, 0.0))
        rows = [spread(panel, j) for j in range(8)]
        if work and t % 2:
            work.pop(0)()
        for s in range(t + 1, count):
            v = tiles[s]
            p = [jnp.broadcast_to(v[:, q + j : q + j + 1], (8, width)) * rows[j] for j in range(8)]
            total = ((p[0] + p[1]) + (p[2] + p[3])) + ((p[4] + p[5]) + (p[6] + p[7]))
            tiles[s] = jnp.where(here, 0.0, v) - total
    return jnp.concatenate(lower, axis=0), jnp.concatenate(scaled, axis=0)


def invert(at_ref, zero_ref, own_ref, other_ref, out_ref, block_ref):
    tiles, half, n = own_ref.shape
    low_is_own = at_ref[0] % 2 == 0
    for t in range(tiles):
        own, other = own_ref[t], other_ref[t]
        low, high = jnp.where(low_is_own, own, other), jnp.where(low_is_own, other, own)
        for j in range(n // 128):
            lanes = slice(128 * j, 128 * j + 128)
            block_ref[j, pl.ds(t, half, stride=tiles), :] = low[:, lanes]
            block_ref[j, pl.ds(t + half * tiles, half, stride=tiles), :] = high[:, lanes]
    for j in range(n // 128):
        out_ref[:, 128 * j : 128 * j + 128] = block_ref[j]
    zero = zero_ref[...]
    work = []
    for lo in range(0, n, BASE):
        own = slice(lo, lo + BASE)
        diagonal = out_ref[own, own]
        lower, scaled = base_factors([diagonal[s : s + 8] for s in range(0, BASE, 8)], zero, work)
        while work:
            work.pop(0)()
        base = across(lower, scaled, ((0,), (0,)), HIGH)
        rows = {c: base if c == lo else across(base, out_ref[own, c : c + BASE], ((1,), (0,)), HIGH) for c in range(0, n, BASE)}
        cols = {r: out_ref[r : r + BASE, own] for r in range(0, n, BASE) if r != lo}

        def product(r, c, lo=lo, rows=rows, cols=cols):
            at = (slice(r, r + BASE), slice(c, c + BASE))
            total = across(cols[r], rows[c], ((1,), (0,)), HIGH)
            out_ref[at] = -total if c == lo else out_ref[at] - total

        for i in range(BASE, n, BASE):
            r = (lo + i) % n
            for c in range(0, n, BASE):
                if r == c == lo + BASE:
                    product(r, c)
                else:
                    work.append(functools.partial(product, r, c))
        for c in range(0, n, BASE):
            out_ref[own, c : c + BASE] = rows[c]
    while work:
        work.pop(0)()


def update(first_ref, at_ref, pruned_ref, inv_ref, near_ref, far_ref, twin_near_ref, twin_far_ref, *refs):
    blocks, (h_ref, w_ref, h_out_ref, w_out_ref, panel_ref, high_ref, low_ref, keep_ref) = refs[:-8], refs[-8:]
    step = pl.program_id(0)
    n = inv_ref.shape[0]
    width = h_ref.shape[1]
    tiles = first_ref.shape[0]
    half = n // tiles
    side = len(blocks) // 2
    block = w_ref.shape[1]
    rows_w = block * pl.num_programs(0)
    apply = ((1,), (0,))

    def cols(start, size):
        return jnp.concatenate([b[:, pl.ds(start, size)] for b in blocks], axis=0)

    @pl.when(step == 0)
    def _():
        core, z = at_ref[0] % 2, at_ref[0] // 2
        near = tiles // 4

        def place(t, _):
            apart = (t // 2) ^ z
            for h in range(2):
                mine = core == h
                of = apart % near * 2 + (t % 2) ^ jnp.where(mine, core, 1 - core)
                kept = jnp.where(apart < near, near_ref[of], far_ref[of])
                sent = jnp.where(apart < near, twin_near_ref[of], twin_far_ref[of])
                place_strips(panel_ref, first_ref[t] + h * half, jnp.where(mine, kept, sent), half, width)
            return 0

        lax.fori_loop(0, tiles, place, 0)
        panel = rows_at(panel_ref, 0, n, width)
        solved = jnp.dot(inv_ref[...], panel, precision=HIGH, preferred_element_type=F32)
        place_rows(panel_ref, 0, 0, solved)
        x, y = at_ref[1] % side, at_ref[1] // side
        hands = []
        for path in range(2):
            for far in range(side):
                for near in range(side):
                    dx, dy = (near, far) if path == 0 else (far, near)
                    hand = (y + side - dy) % side * side + (x + side - dx) % side
                    hands.append(hand + path * (n // 2))
        solved = jnp.concatenate(
            [
                jnp.concatenate([panel_ref[j, pl.ds(h, n // tiles // 2, stride=tiles), :] for h in hands], axis=0)
                for j in range(panel_ref.shape[0])
            ],
            axis=1,
        ).T[:width, :]
        high = solved.astype(BF16)
        high_ref[...] = high
        low_ref[...] = (solved - high.astype(F32)).astype(BF16)
        c_high, c_low = cols(rows_w, width), cols(rows_w + lanes_for(width), width)
        total = across(high_ref[...], c_high, apply)
        total = total + (across(low_ref[...], c_high, apply) + across(high_ref[...], c_low, apply))
        h_out_ref[...] = h_ref[...] - total.T
        unit = lax.broadcasted_iota(jnp.int32, (width, n), 0) + at_ref[1] * width
        hits = jnp.sum(jnp.where(unit == pruned_ref[...], 1.0, 0.0), axis=1, keepdims=True)
        keep_ref[...] = jnp.broadcast_to(1.0 - hits, keep_ref.shape)

    got = cols(pl.multiple_of(step * block, block), block)
    total = across(high_ref[...], got, apply) + across(low_ref[...], got, apply)
    w_out_ref[...] = (w_ref[...].astype(F32) - total) * keep_ref[:, 0:1]


def sent_to_all(copies, axis):
    return lax.all_to_all(copies, axis, split_axis=0, concat_axis=0, tiled=True)


def on_device(hessian_inverse, weights, pruned):
    tile_rows, tile_cols = hessian_inverse.shape
    rows_w = weights.shape[0]
    n = pruned.shape[0]
    tiles = lax.axis_size("row")
    cap = 2 * n // tiles
    half = cap // 2
    at = jnp.stack([lax.axis_index("row"), lax.axis_index("col")]).astype(jnp.int32)
    weights = weights.T
    listed = pruned.reshape(1, n)
    edges = jnp.arange(tiles, dtype=jnp.int32) * tile_cols
    first = jnp.sum((listed < edges[:, None]).astype(jnp.int32), axis=1)
    length = rows_w + 2 * lanes_for(tile_rows)
    hands = pl.pallas_call(
        pack_cols,
        out_shape=jax.ShapeDtypeStruct((8 * tiles, length // 2), BF16),
        in_specs=[SMEM, VMEM, VMEM, VMEM],
        out_specs=VMEM,
        name="pack_cols",
    )(at, listed, hessian_inverse, weights)
    hands = sent_to_all(hands, "col")
    mine = n // tiles
    strips = half * tile_cols // 128
    mine_rows, other_rows = pl.pallas_call(
        pack_rows,
        out_shape=(jax.ShapeDtypeStruct((strips, 128), F32),) * 2,
        in_specs=[SMEM, VMEM, VMEM],
        out_specs=(VMEM, VMEM),
        name="pack_rows",
    )(at, listed, hessian_inverse)

    def swapped(value, mask):
        return lax.ppermute(value, "row", [(i, i ^ mask) for i in range(tiles)])

    rows = jnp.stack([mine_rows, swapped(other_rows, 1)])
    rows = jnp.concatenate([rows, swapped(rows, 2)], axis=0)
    low, high, pieces = pl.pallas_call(
        functools.partial(gather_hand, height=tile_rows, width=tile_cols),
        out_shape=(
            jax.ShapeDtypeStruct((mine // 2, length), BF16),
            jax.ShapeDtypeStruct((mine // 2, length), BF16),
            jax.ShapeDtypeStruct((tiles, cap // 4, 4 * mine), F32),
        ),
        in_specs=[SMEM, VMEM, VMEM],
        out_specs=(VMEM, VMEM, VMEM),
        name="gather_hand",
    )(at, listed, hands)
    pieces = sent_to_all(pieces, "row")
    side = math.isqrt(tiles)

    def along_x(value, d):
        return lax.ppermute(value, "col", [(c, c // side * side + (c + d) % side) for c in range(tiles)])

    def along_y(value, d):
        return lax.ppermute(value, "col", [(c, (c + d * side) % tiles) for c in range(tiles)])

    rows = jnp.concatenate([rows, swapped(rows, 4)], axis=0)
    lows = [low] + [along_x(low, d) for d in range(1, side)]
    highs = [high] + [along_y(high, d) for d in range(1, side)]
    slab = pl.pallas_call(
        pack_slab,
        out_shape=jax.ShapeDtypeStruct((tiles, mine // 2, n), F32),
        in_specs=[SMEM, SMEM, VMEM],
        out_specs=VMEM,
        scratch_shapes=[pltpu.VMEM((n + cap, 128), F32), pltpu.VMEM((mine, n), F32)],
        name="pack_slab",
    )(first, at, pieces)
    slab = sent_to_all(slab, "col")
    low, high = pl.pallas_call(
        join,
        out_shape=(jax.ShapeDtypeStruct((side * mine // 2, length), BF16),) * 2,
        in_specs=[VMEM] * (2 * side),
        out_specs=(VMEM, VMEM),
        name="join",
    )(*lows, *highs)
    cols = [low] + [along_y(low, d) for d in range(1, side)]
    cols += [high] + [along_x(high, d) for d in range(1, side)]
    far_rows = swapped(rows, 8)
    twin_rows = swapped(rows, 1)
    slab_twin = swapped(slab, 1)
    inverse = pl.pallas_call(
        invert,
        out_shape=jax.ShapeDtypeStruct((n, n), F32),
        in_specs=[SMEM, VMEM, VMEM, VMEM],
        out_specs=VMEM,
        scratch_shapes=[pltpu.VMEM((n // 128, n, 128), F32)],
        name="invert",
    )(at, jnp.zeros((8, BASE), F32), slab, slab_twin)
    twin_far = swapped(far_rows, 1)
    steps = 8
    block = rows_w // steps
    whole = lambda shape: pl.BlockSpec(shape, lambda i: (0,) * len(shape), pipeline_mode=pl.Buffered(1))
    strip = pl.BlockSpec((tile_cols, block), lambda i: (0, i))
    h_new, w_new = pl.pallas_call(
        update,
        grid=(steps,),
        out_shape=(
            jax.ShapeDtypeStruct(hessian_inverse.shape, F32),
            jax.ShapeDtypeStruct(weights.shape, F32),
        ),
        in_specs=[SMEM, SMEM] + [whole(a.shape) for a in (listed, inverse, rows, far_rows, twin_rows, twin_far, *cols, hessian_inverse)] + [strip],
        out_specs=(whole(hessian_inverse.shape), strip),
        scratch_shapes=[
            pltpu.VMEM((-(-tile_cols // 128), n + cap, 128), F32),
            pltpu.VMEM((tile_cols, n), BF16),
            pltpu.VMEM((tile_cols, n), BF16),
            pltpu.VMEM((tile_cols, 128), F32),
        ],
        name="update",
    )(
        first, at, listed, inverse, rows, far_rows, twin_rows, twin_far, *cols, hessian_inverse, weights
    )
    return h_new, w_new.T


def solution(mesh):
    specs = (P("row", "col"), P("row", "col"))

    return jax.shard_map(on_device, mesh=mesh, in_specs=(*specs, P()), out_specs=specs, check_vma=False)
```

```python
import functools
import math

import jax
import jax.numpy as jnp
from jax import lax
from jax.experimental import pallas as pl
from jax.experimental.pallas import tpu as pltpu
from jax.sharding import PartitionSpec as P


HIGH = lax.Precision.HIGHEST
F32 = jnp.float32
BF16 = jnp.bfloat16
VMEM = pl.BlockSpec(memory_space=pltpu.VMEM)
SMEM = pl.BlockSpec(memory_space=pltpu.SMEM)
BASE = 128
BLOCK = 256


def across(a, b, dims, precision=None):
    return lax.dot_general(a, b, (dims, ((), ())), precision=precision, preferred_element_type=F32)


def one_hot(index, width):
    slots = index.shape[0]
    return jnp.where(index == lax.broadcasted_iota(jnp.int32, (slots, width), 1), 1.0, 0.0)


def held(pruned, tile, width, place):
    low = tile * width
    before = jnp.sum(jnp.where(pruned < low, 1, 0), axis=1, keepdims=True)
    place = place(before)
    lane = lax.broadcasted_iota(jnp.int32, (place.shape[0], pruned.shape[1]), 1)
    here = (lane == place) & (pruned >= low) & (pruned < low + width)
    return jnp.sum(jnp.where(here, pruned - low + 1, 0), axis=1, keepdims=True) - 1


def in_turn(cap):
    slot = lax.broadcasted_iota(jnp.int32, (cap, 1), 0)
    return lambda before: before + slot


def dealt(before, tiles, slots):
    slot = lax.broadcasted_iota(jnp.int32, (tiles * 2 * slots, 1), 0)
    hand, second, turn = slot // (2 * slots), slot // slots % 2, slot % slots
    return hand, second, (before - hand + tiles - 1) // tiles + turn


def lanes_for(width):
    return -(-width // 128) * 128


def pack_rows(at_ref, pruned_ref, h_ref, rows_ref):
    height = h_ref.shape[0]
    tiles = rows_ref.shape[0]
    cap = 2 * pruned_ref.shape[1] // tiles
    pick = one_hot(held(pruned_ref[...], at_ref[0], height, in_turn(cap)), height)
    rows = across(pick, h_ref[...], ((1,), (0,)), HIGH)
    for core in range(2):
        part = strips_of(rows[cap // 2 * core : cap // 2 * (core + 1)])
        for d in range(core, tiles, 2):
            rows_ref[d] = part


def strips_of(rows):
    count, width = rows.shape
    full = width // 128 * 128
    rest = width - full
    groups = 128 // rest
    each = count // groups
    strips = [rows[:, j : j + 128] for j in range(0, full, 128)]
    strips.append(jnp.concatenate([rows[each * i : each * i + each, full:] for i in range(groups)], axis=1))
    return jnp.concatenate(strips, axis=0)


def place_strips(ref, start, packed, count, width):
    full = width // 128
    rest = width - 128 * full
    each = count * rest // 128
    for j in range(full):
        ref[j, pl.ds(start, count), :] = packed[count * j : count * j + count]
    last = packed[count * full :]
    for i in range(128 // rest):
        ref[full, pl.ds(start + each * i, each), 0:rest] = last[:, rest * i : rest * i + rest]


def pack_cols(at_ref, pruned_ref, h_ref, w_ref, out_ref):
    pruned = pruned_ref[...]
    slots, half = out_ref.shape
    width = h_ref.shape[1]
    tiles = slots // 8
    pick = one_hot(held(pruned, at_ref[1], width, lambda before: dealt_places(before, tiles, 4)), width)
    w = w_ref[...]
    picked = pick.astype(BF16)
    first = across(picked, w[:, :half], ((1,), (0,)))
    last = across(picked, w[:, half:], ((1,), (0,)))
    c = across(pick, h_ref[...], ((1,), (1,)), HIGH)
    c_high = c.astype(BF16).astype(F32)
    spare = jnp.zeros((slots, lanes_for(width) - width), F32)
    last = jnp.concatenate([last, c_high, spare, c - c_high, spare], axis=1)
    second = lax.broadcasted_iota(jnp.int32, (slots, 1), 0) // 4 % 2
    out_ref[...] = jnp.where(second == 1, last, first).astype(BF16)


def dealt_places(before, tiles, slots):
    hand, _, turn = dealt(before, tiles, slots)
    return hand + tiles * turn


def gather_hand(at_ref, pruned_ref, got_ref, low_ref, high_ref, piece_ref, *, height, width):
    pruned = pruned_ref[...]
    slots, half = got_ref.shape
    tiles = piece_ref.shape[0]
    mine = pruned.shape[1] // tiles
    slot = lax.broadcasted_iota(jnp.int32, (slots, 1), 0)
    tile, second, turn = slot // 8, slot // 4 % 2, slot % 4
    before = jnp.sum(jnp.where(pruned < tile * width, 1, 0), axis=1, keepdims=True)
    after = jnp.sum(jnp.where(pruned < tile * width + width, 1, 0), axis=1, keepdims=True)
    hand = at_ref[1]
    turn = (before - hand + tiles - 1) // tiles + turn
    turn = jnp.where(hand + tiles * turn < after, turn, -1)
    got = got_ref[...]
    parts = [
        across(one_hot(jnp.where(second == part, turn, -1), mine).astype(BF16), got, ((0,), (0,)))
        for part in range(2)
    ]
    wide = lanes_for(height)
    c = parts[1][:, half - 2 * wide : half - 2 * wide + height] + parts[1][:, half - wide : half - wide + height]
    cap = 2 * mine
    pick = one_hot(held(pruned, at_ref[0], height, in_turn(cap)), height)
    piece = across(pick, c, ((1,), (1,)), HIGH)
    quarter = cap // 4
    piece = jnp.concatenate([piece[quarter * i : quarter * i + quarter] for i in range(4)], axis=1)
    for d in range(tiles):
        piece_ref[d] = piece
    for part in range(2):
        lanes = slice(half * part, half * part + half)
        low_ref[:, lanes] = parts[part][: mine // 2].astype(BF16)
        high_ref[:, lanes] = parts[part][mine // 2 :].astype(BF16)


def join(*refs):
    count = (len(refs) - 2) // 2
    for path in range(2):
        out = refs[2 * count + path]
        rows = out.shape[0] // count
        for d in range(count):
            out[rows * d : rows * d + rows, :] = refs[count * path + d][...]


def pack_slab(first_ref, at_ref, got_ref, out_ref, slab_ref, turned_ref):
    tiles, quarter, four = got_ref.shape
    mine = four // 4
    for t in range(tiles):
        got = got_ref[t]
        for i in range(4):
            slab_ref[pl.ds(first_ref[t] + quarter * i, quarter), 0:mine] = got[:, mine * i : mine * i + mine]
    turned_ref[...] = slab_ref[0 : turned_ref.shape[1], :].T[0:mine, :]
    half = mine // 2
    slab = turned_ref[pl.ds(pl.multiple_of(at_ref[0] % 2 * half, half), half), :]
    for d in range(tiles):
        out_ref[d] = slab


def spread(v, i):
    return jnp.broadcast_to(v[i : i + 1, :], v.shape)


def base_factors(tiles, zero, work):
    width = tiles[0].shape[1]
    lane = lax.broadcasted_iota(jnp.int32, (8, width), 1)
    sub = lax.broadcasted_iota(jnp.int32, (8, width), 0)
    tiles = list(tiles)
    count = len(tiles)
    lower, scaled = [], []
    for t in range(count):
        q = 8 * t
        own = tiles[t]
        cols = [jnp.broadcast_to(own[:, q + j : q + j + 1], (8, width)) + zero for j in range(8)]
        here = (lane >= q) & (lane < q + 8)
        known = lane < q + 8
        panel = jnp.where(here, jnp.where(lane - q == sub, 1.0, 0.0), own)
        lower.append(jnp.where(known, panel, 0.0))
        for j in range(0, 8, 2):
            k = j + 1
            a, b, b2, c = spread(cols[j], j), spread(cols[k], j), spread(cols[j], k), spread(cols[k], k)
            r = 1.0 / (a * c - b * b2)
            i00, i01, i10, i11 = c * r, -(b * r), -(b2 * r), a * r
            is_j, is_k = sub == j, sub == k
            f_j = jnp.where(is_j, -i00, jnp.where(is_k, -i10, cols[j] * i00 + cols[k] * i10))
            f_k = jnp.where(is_j, -i01, jnp.where(is_k, -i11, cols[j] * i01 + cols[k] * i11))
            pivot = is_j | is_k

            def swept(v):
                return jnp.where(pivot, 0.0, v) - (f_j * spread(v, j) + f_k * spread(v, k))

            for m in range(j + 2, 8):
                cols[m] = swept(cols[m])
            panel = swept(panel)
        scaled.append(jnp.where(known, panel, 0.0))
        rows = [spread(panel, j) for j in range(8)]
        if work and t % 2:
            work.pop(0)()
        for s in range(t + 1, count):
            v = tiles[s]
            p = [jnp.broadcast_to(v[:, q + j : q + j + 1], (8, width)) * rows[j] for j in range(8)]
            total = ((p[0] + p[1]) + (p[2] + p[3])) + ((p[4] + p[5]) + (p[6] + p[7]))
            tiles[s] = jnp.where(here, 0.0, v) - total
    return jnp.concatenate(lower, axis=0), jnp.concatenate(scaled, axis=0)


def invert(at_ref, own_ref, other_ref, out_ref, zero_ref):
    tiles, half, n = own_ref.shape
    low_is_own = at_ref[0] % 2 == 0
    for t in range(tiles):
        own, other = own_ref[t], other_ref[t]
        low, high = jnp.where(low_is_own, own, other), jnp.where(low_is_own, other, own)
        for j in range(n // BASE):
            lanes = slice(BASE * j, BASE * j + BASE)
            out_ref[j, pl.ds(t, half, stride=tiles), :] = low[:, lanes]
            out_ref[j, pl.ds(t + half * tiles, half, stride=tiles), :] = high[:, lanes]
    zero_ref[...] = jnp.zeros_like(zero_ref)
    zero = zero_ref[...]
    blocks = n // BASE
    work = []
    for k in range(blocks):
        own = slice(BASE * k, BASE * k + BASE)
        diagonal = out_ref[k, own, :]
        lower, scaled = base_factors([diagonal[s : s + 8] for s in range(0, BASE, 8)], zero, work)
        while work:
            work.pop(0)()
        base = across(lower, scaled, ((0,), (0,)), HIGH)
        rows = [base if c == k else across(base, out_ref[c, own, :], ((1,), (0,)), HIGH) for c in range(blocks)]
        cols = [out_ref[k, BASE * r : BASE * r + BASE, :] for r in range(blocks)]

        def product(r, c, k=k, rows=rows, cols=cols):
            at = (c, slice(BASE * r, BASE * r + BASE))
            total = across(cols[r], rows[c], ((1,), (0,)), HIGH)
            out_ref[at] = -total if c == k else out_ref[at] - total

        for i in range(1, blocks):
            r = (k + i) % blocks
            for c in range(blocks):
                if r == c == k + 1:
                    product(r, c)
                else:
                    work.append(functools.partial(product, r, c))
        for c in range(blocks):
            out_ref[c, own, :] = rows[c]
    while work:
        work.pop(0)()


def update(first_ref, at_ref, pruned_ref, inv_ref, own_ref, other_ref, *refs):
    blocks, (h_ref, w_ref, h_out, w_out, panel_ref, w_new_ref, h_new_ref, sems) = refs[:-8], refs[-8:]
    strips, n, _ = inv_ref.shape
    width = h_ref.shape[1]
    tiles = first_ref.shape[0]
    half = n // tiles
    side = len(blocks) // 2
    rows_w = w_ref.shape[1]
    steps = rows_w // BLOCK
    low_is_own = at_ref[0] % 2 == 0
    for t in range(tiles):
        own, other = own_ref[t], other_ref[t]
        place_strips(panel_ref, first_ref[t], jnp.where(low_is_own, own, other), half, width)
        place_strips(panel_ref, first_ref[t] + half, jnp.where(low_is_own, other, own), half, width)
    panel = jnp.concatenate([panel_ref[j, 0:n, :] for j in range(panel_ref.shape[0])], axis=1).T[:width, :]
    x, y = at_ref[1] % side, at_ref[1] // side
    hands = []
    for path in range(2):
        for far in range(side):
            for near in range(side):
                dx, dy = (near, far) if path == 0 else (far, near)
                hand = (y + side - dy) % side * side + (x + side - dx) % side
                hands.append(hand + path * (n // 2))
    inverse = jnp.concatenate(
        [
            jnp.concatenate([inv_ref[j, pl.ds(h, n // tiles // 2, stride=tiles), :] for h in hands], axis=0)
            for j in range(strips)
        ],
        axis=1,
    )
    solved = across(panel, inverse, ((1,), (1,)), HIGH)
    high = solved.astype(BF16)
    low = (solved - high.astype(F32)).astype(BF16)
    unit = lax.broadcasted_iota(jnp.int32, (width, n), 0) + at_ref[1] * width
    keep = 1.0 - jnp.sum(jnp.where(unit == pruned_ref[...], 1.0, 0.0), axis=1, keepdims=True)
    apply = ((1,), (0,))

    def cols(start, size):
        return jnp.concatenate([b[:, start : start + size] for b in blocks], axis=0)

    copies = []
    for i in range(steps):
        at = slice(BLOCK * i, BLOCK * i + BLOCK)
        got = cols(BLOCK * i, BLOCK)
        total = across(high, got, apply) + across(low, got, apply)
        w_new_ref[:, at] = (w_ref[:, at].astype(F32) - total) * keep
        copies.append(pltpu.make_async_copy(w_new_ref.at[:, at], w_out.at[:, at], sems.at[i]))
        copies[-1].start()
    c_high, c_low = cols(rows_w, width), cols(rows_w + lanes_for(width), width)
    total = across(high, c_high, apply) + (across(low, c_high, apply) + across(high, c_low, apply))
    h_new_ref[...] = h_ref[...] - total.T
    copies.append(pltpu.make_async_copy(h_new_ref, h_out, sems.at[steps]))
    copies[-1].start()
    for copy in copies:
        copy.wait()


def sent_to_all(copies, axis):
    return lax.all_to_all(copies, axis, split_axis=0, concat_axis=0, tiled=True)


def on_device(hessian_inverse, weights, pruned):
    tile_rows, tile_cols = hessian_inverse.shape
    rows_w = weights.shape[0]
    n = pruned.shape[0]
    tiles = lax.axis_size("row")
    cap = 2 * n // tiles
    half = cap // 2
    at = jnp.stack([lax.axis_index("row"), lax.axis_index("col")]).astype(jnp.int32)
    weights = weights.T
    listed = pruned.reshape(1, n)
    edges = jnp.arange(tiles, dtype=jnp.int32) * tile_cols
    first = jnp.sum((listed < edges[:, None]).astype(jnp.int32), axis=1)
    length = rows_w + 2 * lanes_for(tile_rows)
    hands = pl.pallas_call(
        pack_cols,
        out_shape=jax.ShapeDtypeStruct((8 * tiles, length // 2), BF16),
        in_specs=[SMEM, VMEM, VMEM, VMEM],
        out_specs=VMEM,
        name="pack_cols",
    )(at, listed, hessian_inverse, weights)
    hands = sent_to_all(hands, "col")
    mine = n // tiles
    rows = pl.pallas_call(
        pack_rows,
        out_shape=jax.ShapeDtypeStruct((tiles, half * tile_cols // 128, 128), F32),
        in_specs=[SMEM, VMEM, VMEM],
        out_specs=VMEM,
        name="pack_rows",
    )(at, listed, hessian_inverse)

    def swapped(value, mask):
        return lax.ppermute(value, "row", [(i, i ^ mask) for i in range(tiles)])

    low, high, pieces = pl.pallas_call(
        functools.partial(gather_hand, height=tile_rows, width=tile_cols),
        out_shape=(
            jax.ShapeDtypeStruct((mine // 2, length), BF16),
            jax.ShapeDtypeStruct((mine // 2, length), BF16),
            jax.ShapeDtypeStruct((tiles, cap // 4, 4 * mine), F32),
        ),
        in_specs=[SMEM, VMEM, VMEM],
        out_specs=(VMEM, VMEM, VMEM),
        name="gather_hand",
    )(at, listed, hands)
    pieces = sent_to_all(pieces, "row")
    side = math.isqrt(tiles)

    def along_x(value, d):
        return lax.ppermute(value, "col", [(c, c // side * side + (c + d) % side) for c in range(tiles)])

    def along_y(value, d):
        return lax.ppermute(value, "col", [(c, (c + d * side) % tiles) for c in range(tiles)])

    lows = [low] + [along_x(low, d) for d in range(1, side)]
    highs = [high] + [along_y(high, d) for d in range(1, side)]
    slab = pl.pallas_call(
        pack_slab,
        out_shape=jax.ShapeDtypeStruct((tiles, mine // 2, n), F32),
        in_specs=[SMEM, SMEM, VMEM],
        out_specs=VMEM,
        scratch_shapes=[pltpu.VMEM((n + cap, 128), F32), pltpu.VMEM((mine, n), F32)],
        name="pack_slab",
    )(first, at, pieces)
    slab = sent_to_all(slab, "col")
    low, high = pl.pallas_call(
        join,
        out_shape=(jax.ShapeDtypeStruct((side * mine // 2, length), BF16),) * 2,
        in_specs=[VMEM] * (2 * side),
        out_specs=(VMEM, VMEM),
        name="join",
    )(*lows, *highs)
    cols = [low] + [along_y(low, d) for d in range(1, side)]
    cols += [high] + [along_x(high, d) for d in range(1, side)]
    rows = sent_to_all(rows, "row")
    slab_twin = swapped(slab, 1)
    inverse = pl.pallas_call(
        invert,
        out_shape=jax.ShapeDtypeStruct((n // BASE, n, BASE), F32),
        in_specs=[SMEM, VMEM, VMEM],
        out_specs=VMEM,
        scratch_shapes=[pltpu.VMEM((8, BASE), F32)],
        name="invert",
    )(at, slab, slab_twin)
    rows_twin = swapped(rows, 1)
    anywhere = pl.BlockSpec(memory_space=pl.ANY)
    h_new, w_new = pl.pallas_call(
        update,
        out_shape=(
            jax.ShapeDtypeStruct(hessian_inverse.shape, F32),
            jax.ShapeDtypeStruct(weights.shape, F32),
        ),
        in_specs=[SMEM, SMEM] + [VMEM] * (6 + len(cols)),
        out_specs=(anywhere, anywhere),
        scratch_shapes=[
            pltpu.VMEM((-(-tile_cols // 128), n + cap, 128), F32),
            pltpu.VMEM(weights.shape, F32),
            pltpu.VMEM(hessian_inverse.shape, F32),
            pltpu.SemaphoreType.DMA((rows_w // BLOCK + 1,)),
        ],
        name="update",
    )(first, at, listed, inverse, rows, rows_twin, *cols, hessian_inverse, weights)
    return h_new, w_new.T


def solution(mesh):
    specs = (P("row", "col"), P("row", "col"))

    return jax.shard_map(on_device, mesh=mesh, in_specs=(*specs, P()), out_specs=specs, check_vma=False)
```

```python
import functools
import math

import jax
import jax.numpy as jnp
from jax import lax
from jax.experimental import pallas as pl
from jax.experimental.pallas import tpu as pltpu
from jax.sharding import PartitionSpec as P


HIGH = lax.Precision.HIGHEST
F32 = jnp.float32
BF16 = jnp.bfloat16
VMEM = pl.BlockSpec(memory_space=pltpu.VMEM)
SMEM = pl.BlockSpec(memory_space=pltpu.SMEM)
BASE = 128
BLOCK = 256


def across(a, b, dims, precision=None):
    return lax.dot_general(a, b, (dims, ((), ())), precision=precision, preferred_element_type=F32)


def one_hot(index, width):
    slots = index.shape[0]
    return jnp.where(index == lax.broadcasted_iota(jnp.int32, (slots, width), 1), 1.0, 0.0)


def held(pruned, tile, width, place):
    low = tile * width
    before = jnp.sum(jnp.where(pruned < low, 1, 0), axis=1, keepdims=True)
    place = place(before)
    lane = lax.broadcasted_iota(jnp.int32, (place.shape[0], pruned.shape[1]), 1)
    here = (lane == place) & (pruned >= low) & (pruned < low + width)
    return jnp.sum(jnp.where(here, pruned - low + 1, 0), axis=1, keepdims=True) - 1


def in_turn(cap):
    slot = lax.broadcasted_iota(jnp.int32, (cap, 1), 0)
    return lambda before: before + slot


def dealt(before, tiles, slots):
    slot = lax.broadcasted_iota(jnp.int32, (tiles * 2 * slots, 1), 0)
    hand, second, turn = slot // (2 * slots), slot // slots % 2, slot % slots
    return hand, second, (before - hand + tiles - 1) // tiles + turn


def lanes_for(width):
    return -(-width // 128) * 128


def pack_rows(at_ref, pruned_ref, h_ref, rows_ref):
    height, width = h_ref.shape
    cap = rows_ref.shape[0] * 128 // width
    pick = one_hot(held(pruned_ref[...], at_ref[0], height, in_turn(cap)), height)
    rows_ref[...] = strips_of(across(pick, h_ref[...], ((1,), (0,)), HIGH))


def strips_of(rows):
    count, width = rows.shape
    full = width // 128 * 128
    rest = width - full
    groups = 128 // rest
    each = count // groups
    strips = [rows[:, j : j + 128] for j in range(0, full, 128)]
    strips.append(jnp.concatenate([rows[each * i : each * i + each, full:] for i in range(groups)], axis=1))
    return jnp.concatenate(strips, axis=0)


def place_strips(ref, start, packed, count, width):
    full = width // 128
    rest = width - 128 * full
    each = count * rest // 128
    for j in range(full):
        ref[j, pl.ds(start, count), :] = packed[count * j : count * j + count]
    last = packed[count * full :]
    for i in range(128 // rest):
        ref[full, pl.ds(start + each * i, each), 0:rest] = last[:, rest * i : rest * i + rest]


def pack_cols(at_ref, pruned_ref, h_ref, w_ref, out_ref):
    pruned = pruned_ref[...]
    slots, half = out_ref.shape
    width = h_ref.shape[1]
    tiles = slots // 8
    pick = one_hot(held(pruned, at_ref[1], width, lambda before: dealt_places(before, tiles, 4)), width)
    w = w_ref[...]
    picked = pick.astype(BF16)
    first = across(picked, w[:, :half], ((1,), (0,)))
    last = across(picked, w[:, half:], ((1,), (0,)))
    c = across(pick, h_ref[...], ((1,), (1,)), HIGH)
    c_high = c.astype(BF16).astype(F32)
    spare = jnp.zeros((slots, lanes_for(width) - width), F32)
    last = jnp.concatenate([last, c_high, spare, c - c_high, spare], axis=1)
    second = lax.broadcasted_iota(jnp.int32, (slots, 1), 0) // 4 % 2
    out_ref[...] = jnp.where(second == 1, last, first).astype(BF16)


def dealt_places(before, tiles, slots):
    hand, _, turn = dealt(before, tiles, slots)
    return hand + tiles * turn


def gather_hand(at_ref, pruned_ref, got_ref, low_ref, high_ref, piece_ref, *, height, width):
    pruned = pruned_ref[...]
    slots, half = got_ref.shape
    tiles = piece_ref.shape[0]
    mine = pruned.shape[1] // tiles
    slot = lax.broadcasted_iota(jnp.int32, (slots, 1), 0)
    tile, second, turn = slot // 8, slot // 4 % 2, slot % 4
    before = jnp.sum(jnp.where(pruned < tile * width, 1, 0), axis=1, keepdims=True)
    after = jnp.sum(jnp.where(pruned < tile * width + width, 1, 0), axis=1, keepdims=True)
    hand = at_ref[1]
    turn = (before - hand + tiles - 1) // tiles + turn
    turn = jnp.where(hand + tiles * turn < after, turn, -1)
    got = got_ref[...]
    parts = [
        across(one_hot(jnp.where(second == part, turn, -1), mine).astype(BF16), got, ((0,), (0,)))
        for part in range(2)
    ]
    wide = lanes_for(height)
    c = parts[1][:, half - 2 * wide : half - 2 * wide + height] + parts[1][:, half - wide : half - wide + height]
    cap = 2 * mine
    pick = one_hot(held(pruned, at_ref[0], height, in_turn(cap)), height)
    piece = across(pick, c, ((1,), (1,)), HIGH)
    for core in range(2):
        part = piece[:, mine // 2 * core : mine // 2 * (core + 1)]
        part = jnp.concatenate([part[8 * i : 8 * i + 8] for i in range(cap // 8)], axis=1)
        for d in range(core, tiles, 2):
            piece_ref[d] = part
    for part in range(2):
        lanes = slice(half * part, half * part + half)
        low_ref[:, lanes] = parts[part][: mine // 2].astype(BF16)
        high_ref[:, lanes] = parts[part][mine // 2 :].astype(BF16)


def join(*refs):
    count = (len(refs) - 2) // 2
    for path in range(2):
        out = refs[2 * count + path]
        rows = out.shape[0] // count
        for d in range(count):
            out[rows * d : rows * d + rows, :] = refs[count * path + d][...]


def pack_slab(first_ref, got_ref, out_ref, slab_ref):
    tiles, mine, n = out_ref.shape
    groups = got_ref.shape[2] // mine
    for t in range(tiles):
        got = got_ref[t]
        for i in range(groups):
            slab_ref[pl.ds(first_ref[t] + 8 * i, 8), 0:mine] = got[:, mine * i : mine * i + mine]
    slab = slab_ref[0:n, :].T[0:mine, :]
    for d in range(tiles):
        out_ref[d] = slab


def spread(v, i):
    return jnp.broadcast_to(v[i : i + 1, :], v.shape)


def base_factors(tiles, zero, work):
    width = tiles[0].shape[1]
    lane = lax.broadcasted_iota(jnp.int32, (8, width), 1)
    sub = lax.broadcasted_iota(jnp.int32, (8, width), 0)
    tiles = list(tiles)
    count = len(tiles)
    lower, scaled = [], []
    for t in range(count):
        q = 8 * t
        own = tiles[t]
        cols = [jnp.broadcast_to(own[:, q + j : q + j + 1], (8, width)) + zero for j in range(8)]
        here = (lane >= q) & (lane < q + 8)
        known = lane < q + 8
        panel = jnp.where(here, jnp.where(lane - q == sub, 1.0, 0.0), own)
        lower.append(jnp.where(known, panel, 0.0))
        for j in range(0, 8, 2):
            k = j + 1
            a, b, b2, c = spread(cols[j], j), spread(cols[k], j), spread(cols[j], k), spread(cols[k], k)
            r = 1.0 / (a * c - b * b2)
            i00, i01, i10, i11 = c * r, -(b * r), -(b2 * r), a * r
            is_j, is_k = sub == j, sub == k
            f_j = jnp.where(is_j, -i00, jnp.where(is_k, -i10, cols[j] * i00 + cols[k] * i10))
            f_k = jnp.where(is_j, -i01, jnp.where(is_k, -i11, cols[j] * i01 + cols[k] * i11))
            pivot = is_j | is_k

            def swept(v):
                return jnp.where(pivot, 0.0, v) - (f_j * spread(v, j) + f_k * spread(v, k))

            for m in range(j + 2, 8):
                cols[m] = swept(cols[m])
            panel = swept(panel)
        scaled.append(jnp.where(known, panel, 0.0))
        rows = [spread(panel, j) for j in range(8)]
        if work:
            work.pop(0)()
        for s in range(t + 1, count):
            v = tiles[s]
            p = [jnp.broadcast_to(v[:, q + j : q + j + 1], (8, width)) * rows[j] for j in range(8)]
            total = ((p[0] + p[1]) + (p[2] + p[3])) + ((p[4] + p[5]) + (p[6] + p[7]))
            tiles[s] = jnp.where(here, 0.0, v) - total
    return jnp.concatenate(lower, axis=0), jnp.concatenate(scaled, axis=0)


def invert(at_ref, own_ref, other_ref, out_ref, zero_ref):
    tiles, half, n = own_ref.shape
    low_is_own = at_ref[0] % 2 == 0
    for t in range(tiles):
        own, other = own_ref[t], other_ref[t]
        low, high = jnp.where(low_is_own, own, other), jnp.where(low_is_own, other, own)
        for j in range(n // BASE):
            lanes = slice(BASE * j, BASE * j + BASE)
            out_ref[j, pl.ds(t, half, stride=tiles), :] = low[:, lanes]
            out_ref[j, pl.ds(t + half * tiles, half, stride=tiles), :] = high[:, lanes]
    zero_ref[...] = jnp.zeros_like(zero_ref)
    zero = zero_ref[...]
    blocks = n // BASE
    work = []
    for k in range(blocks):
        own = slice(BASE * k, BASE * k + BASE)
        diagonal = out_ref[k, own, :]
        lower, scaled = base_factors([diagonal[s : s + 8] for s in range(0, BASE, 8)], zero, work)
        while work:
            work.pop(0)()
        base = across(lower, scaled, ((0,), (0,)), HIGH)
        rows = {k: base}
        cols = [out_ref[k, BASE * r : BASE * r + BASE, :] for r in range(blocks)]
        out_ref[k, own, :] = base

        def row(c, own=own, rows=rows, base=base):
            rows[c] = across(base, out_ref[c, own, :], ((1,), (0,)), HIGH)
            out_ref[c, own, :] = rows[c]

        def product(r, c, k=k, rows=rows, cols=cols):
            at = (c, slice(BASE * r, BASE * r + BASE))
            total = across(cols[r], rows[c], ((1,), (0,)), HIGH)
            out_ref[at] = -total if c == k else out_ref[at] - total

        following = (k + 1) % blocks
        if k + 1 < blocks:
            row(following)
            product(following, following)
        for c in [(k + i) % blocks for i in range(1, blocks)]:
            if c != following or k + 1 == blocks:
                work.append(functools.partial(row, c))
        for c in [(k + i) % blocks for i in range(1, blocks + 1)]:
            for r in [(k + i) % blocks for i in range(1, blocks)]:
                if not r == c == k + 1:
                    work.append(functools.partial(product, r, c))
    while work:
        work.pop(0)()


def update(first_ref, at_ref, pruned_ref, inv_ref, near_ref, far_ref, twin_near_ref, twin_far_ref, *refs):
    blocks, (h_ref, w_ref, h_out, w_out, panel_ref, w_new_ref, h_new_ref, sems) = refs[:-8], refs[-8:]
    strips, n, _ = inv_ref.shape
    width = h_ref.shape[1]
    tiles = first_ref.shape[0]
    cap = 2 * n // tiles
    side = len(blocks) // 2
    rows_w = w_ref.shape[1]
    steps = rows_w // BLOCK
    core, z = at_ref[0] % 2, at_ref[0] // 2
    near = near_ref.shape[0]
    for t in range(tiles):
        apart = (t // 2) ^ z
        of = apart % near
        own = jnp.where(apart < near, near_ref[of], far_ref[of])
        twin = jnp.where(apart < near, twin_near_ref[of], twin_far_ref[of])
        place_strips(panel_ref, first_ref[t], jnp.where(core == t % 2, own, twin), cap, width)
    panel = jnp.concatenate([panel_ref[j, 0:n, :] for j in range(panel_ref.shape[0])], axis=1).T[:width, :]
    x, y = at_ref[1] % side, at_ref[1] // side
    hands = []
    for path in range(2):
        for far in range(side):
            for near in range(side):
                dx, dy = (near, far) if path == 0 else (far, near)
                hand = (y + side - dy) % side * side + (x + side - dx) % side
                hands.append(hand + path * (n // 2))
    inverse = jnp.concatenate(
        [
            jnp.concatenate([inv_ref[j, pl.ds(h, n // tiles // 2, stride=tiles), :] for h in hands], axis=0)
            for j in range(strips)
        ],
        axis=1,
    )
    solved = across(panel, inverse, ((1,), (1,)), HIGH)
    high = solved.astype(BF16)
    low = (solved - high.astype(F32)).astype(BF16)
    unit = lax.broadcasted_iota(jnp.int32, (width, n), 0) + at_ref[1] * width
    keep = 1.0 - jnp.sum(jnp.where(unit == pruned_ref[...], 1.0, 0.0), axis=1, keepdims=True)
    apply = ((1,), (0,))

    def cols(start, size):
        return jnp.concatenate([b[:, start : start + size] for b in blocks], axis=0)

    copies = []
    for i in range(steps):
        at = slice(BLOCK * i, BLOCK * i + BLOCK)
        got = cols(BLOCK * i, BLOCK)
        total = across(high, got, apply) + across(low, got, apply)
        w_new_ref[:, at] = (w_ref[:, at].astype(F32) - total) * keep
        copies.append(pltpu.make_async_copy(w_new_ref.at[:, at], w_out.at[:, at], sems.at[i]))
        copies[-1].start()
    c_high, c_low = cols(rows_w, width), cols(rows_w + lanes_for(width), width)
    total = across(high, c_high, apply) + (across(low, c_high, apply) + across(high, c_low, apply))
    h_new_ref[...] = h_ref[...] - total.T
    copies.append(pltpu.make_async_copy(h_new_ref, h_out, sems.at[steps]))
    copies[-1].start()
    for copy in copies:
        copy.wait()


def sent_to_all(copies, axis):
    return lax.all_to_all(copies, axis, split_axis=0, concat_axis=0, tiled=True)


def on_device(hessian_inverse, weights, pruned):
    tile_rows, tile_cols = hessian_inverse.shape
    rows_w = weights.shape[0]
    n = pruned.shape[0]
    tiles = lax.axis_size("row")
    cap = 2 * n // tiles
    at = jnp.stack([lax.axis_index("row"), lax.axis_index("col")]).astype(jnp.int32)
    weights = weights.T
    listed = pruned.reshape(1, n)
    edges = jnp.arange(tiles, dtype=jnp.int32) * tile_cols
    first = jnp.sum((listed < edges[:, None]).astype(jnp.int32), axis=1)
    length = rows_w + 2 * lanes_for(tile_rows)
    hands = pl.pallas_call(
        pack_cols,
        out_shape=jax.ShapeDtypeStruct((8 * tiles, length // 2), BF16),
        in_specs=[SMEM, VMEM, VMEM, VMEM],
        out_specs=VMEM,
        name="pack_cols",
    )(at, listed, hessian_inverse, weights)
    hands = sent_to_all(hands, "col")
    mine = n // tiles
    rows = pl.pallas_call(
        pack_rows,
        out_shape=jax.ShapeDtypeStruct((cap * tile_cols // 128, 128), F32),
        in_specs=[SMEM, VMEM, VMEM],
        out_specs=VMEM,
        name="pack_rows",
    )(at, listed, hessian_inverse)

    def swapped(value, mask):
        return lax.ppermute(value, "row", [(i, i ^ mask) for i in range(tiles)])

    near_rows = [rows] + [swapped(rows, 2 * m) for m in range(1, 4)]
    near_rows = jnp.stack(near_rows)
    low, high, pieces = pl.pallas_call(
        functools.partial(gather_hand, height=tile_rows, width=tile_cols),
        out_shape=(
            jax.ShapeDtypeStruct((mine // 2, length), BF16),
            jax.ShapeDtypeStruct((mine // 2, length), BF16),
            jax.ShapeDtypeStruct((tiles, 8, cap // 8 * (mine // 2)), F32),
        ),
        in_specs=[SMEM, VMEM, VMEM],
        out_specs=(VMEM, VMEM, VMEM),
        name="gather_hand",
    )(at, listed, hands)
    pieces = sent_to_all(pieces, "row")
    side = math.isqrt(tiles)

    def along_x(value, d):
        return lax.ppermute(value, "col", [(c, c // side * side + (c + d) % side) for c in range(tiles)])

    def along_y(value, d):
        return lax.ppermute(value, "col", [(c, (c + d * side) % tiles) for c in range(tiles)])

    lows = [low] + [along_x(low, d) for d in range(1, side)]
    highs = [high] + [along_y(high, d) for d in range(1, side)]
    slab = pl.pallas_call(
        pack_slab,
        out_shape=jax.ShapeDtypeStruct((tiles, mine // 2, n), F32),
        in_specs=[SMEM, VMEM],
        out_specs=VMEM,
        scratch_shapes=[pltpu.VMEM((n + cap, 128), F32)],
        name="pack_slab",
    )(first, pieces)
    slab = sent_to_all(slab, "col")
    low, high = pl.pallas_call(
        join,
        out_shape=(jax.ShapeDtypeStruct((side * mine // 2, length), BF16),) * 2,
        in_specs=[VMEM] * (2 * side),
        out_specs=(VMEM, VMEM),
        name="join",
    )(*lows, *highs)
    cols = [low] + [along_y(low, d) for d in range(1, side)]
    cols += [high] + [along_x(high, d) for d in range(1, side)]
    far_rows = swapped(near_rows, 8)
    twin_near = swapped(near_rows, 1)
    slab_twin = swapped(slab, 1)
    inverse = pl.pallas_call(
        invert,
        out_shape=jax.ShapeDtypeStruct((n // BASE, n, BASE), F32),
        in_specs=[SMEM, VMEM, VMEM],
        out_specs=VMEM,
        scratch_shapes=[pltpu.VMEM((8, BASE), F32)],
        name="invert",
    )(at, slab, slab_twin)
    twin_far = swapped(far_rows, 1)
    anywhere = pl.BlockSpec(memory_space=pl.ANY)
    h_new, w_new = pl.pallas_call(
        update,
        out_shape=(
            jax.ShapeDtypeStruct(hessian_inverse.shape, F32),
            jax.ShapeDtypeStruct(weights.shape, F32),
        ),
        in_specs=[SMEM, SMEM] + [VMEM] * (8 + len(cols)),
        out_specs=(anywhere, anywhere),
        scratch_shapes=[
            pltpu.VMEM((-(-tile_cols // 128), n + cap, 128), F32),
            pltpu.VMEM(weights.shape, F32),
            pltpu.VMEM(hessian_inverse.shape, F32),
            pltpu.SemaphoreType.DMA((rows_w // BLOCK + 1,)),
        ],
        name="update",
    )(
        first, at, listed, inverse, near_rows, far_rows, twin_near, twin_far, *cols, hessian_inverse, weights
    )
    return h_new, w_new.T


def solution(mesh):
    specs = (P("row", "col"), P("row", "col"))

    return jax.shard_map(on_device, mesh=mesh, in_specs=(*specs, P()), out_specs=specs, check_vma=False)
```

```python
import functools
import math

import jax
import jax.numpy as jnp
from jax import lax
from jax.experimental import pallas as pl
from jax.experimental.pallas import tpu as pltpu
from jax.sharding import PartitionSpec as P


HIGH = lax.Precision.HIGHEST
F32 = jnp.float32
BF16 = jnp.bfloat16
VMEM = pl.BlockSpec(memory_space=pltpu.VMEM)
SMEM = pl.BlockSpec(memory_space=pltpu.SMEM)
ANY = pl.BlockSpec(memory_space=pl.ANY)
BASE = 128
BLOCK = 256


def across(a, b, dims, precision=None):
    return lax.dot_general(a, b, (dims, ((), ())), precision=precision, preferred_element_type=F32)


def one_hot(index, width):
    slots = index.shape[0]
    return jnp.where(index == lax.broadcasted_iota(jnp.int32, (slots, width), 1), 1.0, 0.0)


def held(pruned, tile, width, place):
    low = tile * width
    before = jnp.sum(jnp.where(pruned < low, 1, 0), axis=1, keepdims=True)
    place = place(before)
    lane = lax.broadcasted_iota(jnp.int32, (place.shape[0], pruned.shape[1]), 1)
    here = (lane == place) & (pruned >= low) & (pruned < low + width)
    return jnp.sum(jnp.where(here, pruned - low + 1, 0), axis=1, keepdims=True) - 1


def in_turn(cap):
    slot = lax.broadcasted_iota(jnp.int32, (cap, 1), 0)
    return lambda before: before + slot


def dealt(before, tiles, slots):
    slot = lax.broadcasted_iota(jnp.int32, (tiles * 2 * slots, 1), 0)
    hand, second, turn = slot // (2 * slots), slot // slots % 2, slot % slots
    return hand, second, (before - hand + tiles - 1) // tiles + turn


def lanes_for(width):
    return -(-width // 128) * 128


def pack_rows(at_ref, pruned_ref, h_ref, rows_ref):
    height, width = h_ref.shape
    cap = rows_ref.shape[0] * 128 // width
    pick = one_hot(held(pruned_ref[...], at_ref[0], height, in_turn(cap)), height)
    rows_ref[...] = strips_of(across(pick, h_ref[...], ((1,), (0,)), HIGH))


def strips_of(rows):
    count, width = rows.shape
    full = width // 128 * 128
    rest = width - full
    groups = 128 // rest
    each = count // groups
    strips = [rows[:, j : j + 128] for j in range(0, full, 128)]
    strips.append(jnp.concatenate([rows[each * i : each * i + each, full:] for i in range(groups)], axis=1))
    return jnp.concatenate(strips, axis=0)


def place_strips(ref, start, packed, count, width):
    full = width // 128
    rest = width - 128 * full
    each = count * rest // 128
    for j in range(full):
        ref[j, pl.ds(start, count), :] = packed[count * j : count * j + count]
    last = packed[count * full :]
    for i in range(128 // rest):
        ref[full, pl.ds(start + each * i, each), 0:rest] = last[:, rest * i : rest * i + rest]


def pack_cols(pruned_ref, h_hbm, w_hbm, out_ref, h_ref, w_ref, sems):
    slots, half = out_ref.shape
    copies = [
        pltpu.make_async_copy(h_hbm, h_ref, sems.at[0]),
        pltpu.make_async_copy(w_hbm.at[:, half:], w_ref.at[:, half:], sems.at[1]),
        pltpu.make_async_copy(w_hbm.at[:, :half], w_ref.at[:, :half], sems.at[2]),
    ]
    for copy in copies:
        copy.start()
    pruned = pruned_ref[...]
    width = h_ref.shape[1]
    tiles = slots // 8
    pick = one_hot(held(pruned, lax.axis_index("col"), width, lambda before: dealt_places(before, tiles, 4)), width)
    picked = pick.astype(BF16)
    copies[0].wait()
    c = across(pick, h_ref[...], ((1,), (1,)), HIGH)
    c_high = c.astype(BF16).astype(F32)
    copies[1].wait()
    last = across(picked, w_ref[:, half:], ((1,), (0,)))
    spare = jnp.zeros((slots, lanes_for(width) - width), F32)
    last = jnp.concatenate([last, c_high, spare, c - c_high, spare], axis=1)
    second = lax.broadcasted_iota(jnp.int32, (slots, 1), 0) // 4 % 2
    copies[2].wait()
    first = across(picked, w_ref[:, :half], ((1,), (0,)))
    out_ref[...] = jnp.where(second == 1, last, first).astype(BF16)


def dealt_places(before, tiles, slots):
    hand, _, turn = dealt(before, tiles, slots)
    return hand + tiles * turn


def gather_hand(at_ref, pruned_ref, sent_ref, low_ref, high_ref, piece_ref, got_ref, sem, *, height, width):
    copy = pltpu.make_async_copy(sent_ref, got_ref, sem)
    copy.start()
    pruned = pruned_ref[...]
    slots, half = got_ref.shape
    tiles = piece_ref.shape[0]
    mine = pruned.shape[1] // tiles
    slot = lax.broadcasted_iota(jnp.int32, (slots, 1), 0)
    tile, second, turn = slot // 8, slot // 4 % 2, slot % 4
    before = jnp.sum(jnp.where(pruned < tile * width, 1, 0), axis=1, keepdims=True)
    after = jnp.sum(jnp.where(pruned < tile * width + width, 1, 0), axis=1, keepdims=True)
    hand = at_ref[1]
    turn = (before - hand + tiles - 1) // tiles + turn
    turn = jnp.where(hand + tiles * turn < after, turn, -1)
    cap = 2 * mine
    pick = one_hot(held(pruned, at_ref[0], height, in_turn(cap)), height)
    deal = [one_hot(jnp.where(second == part, turn, -1), mine).astype(BF16) for part in range(2)]
    copy.wait()
    got = got_ref[...]
    parts = [across(d, got, ((0,), (0,))) for d in deal]
    wide = lanes_for(height)
    c = parts[1][:, half - 2 * wide : half - 2 * wide + height] + parts[1][:, half - wide : half - wide + height]
    piece = across(pick, c, ((1,), (1,)), HIGH)
    for core in range(2):
        part = piece[:, mine // 2 * core : mine // 2 * (core + 1)]
        part = jnp.concatenate([part[8 * i : 8 * i + 8] for i in range(cap // 8)], axis=1)
        for d in range(core, tiles, 2):
            piece_ref[d] = part
    for part in range(2):
        lanes = slice(half * part, half * part + half)
        low_ref[:, lanes] = parts[part][: mine // 2].astype(BF16)
        high_ref[:, lanes] = parts[part][mine // 2 :].astype(BF16)


def join(*refs):
    count = (len(refs) - 3) // 2
    sems = refs[-1]
    copies = []
    for path in range(2):
        out = refs[2 * count + path]
        rows = out.shape[0] // count
        for d in range(count):
            i = count * path + d
            copies.append(pltpu.make_async_copy(refs[i], out.at[rows * d : rows * d + rows, :], sems.at[i]))
            copies[-1].start()
    for copy in copies:
        copy.wait()


def pack_slab(pruned_ref, got_ref, out_ref, slab_ref, *, width):
    tiles, mine, n = out_ref.shape
    groups = got_ref.shape[2] // mine
    first = first_places(pruned_ref[...], tiles, width)
    for t in range(tiles):
        got = got_ref[t]
        for i in range(groups):
            slab_ref[pl.ds(first[t] + 8 * i, 8), 0:mine] = got[:, mine * i : mine * i + mine]
    slab = slab_ref[0:n, :].T[0:mine, :]
    for d in range(tiles):
        out_ref[d] = slab


def first_places(pruned, tiles, width):
    return [jnp.sum(jnp.where(pruned < t * width, 1, 0)) for t in range(tiles)]


def spread(v, i):
    return jnp.broadcast_to(v[i : i + 1, :], v.shape)


def base_factors(tiles, zero, work):
    width = tiles[0].shape[1]
    lane = lax.broadcasted_iota(jnp.int32, (8, width), 1)
    sub = lax.broadcasted_iota(jnp.int32, (8, width), 0)
    tiles = list(tiles)
    count = len(tiles)
    lower, scaled = [], []
    for t in range(count):
        q = 8 * t
        own = tiles[t]
        cols = [jnp.broadcast_to(own[:, q + j : q + j + 1], (8, width)) + zero for j in range(8)]
        here = (lane >= q) & (lane < q + 8)
        known = lane < q + 8
        panel = jnp.where(here, jnp.where(lane - q == sub, 1.0, 0.0), own)
        lower.append(jnp.where(known, panel, 0.0))
        for j in range(0, 8, 2):
            k = j + 1
            a, b, b2, c = spread(cols[j], j), spread(cols[k], j), spread(cols[j], k), spread(cols[k], k)
            r = 1.0 / (a * c - b * b2)
            i00, i01, i10, i11 = c * r, -(b * r), -(b2 * r), a * r
            is_j, is_k = sub == j, sub == k
            f_j = jnp.where(is_j, -i00, jnp.where(is_k, -i10, cols[j] * i00 + cols[k] * i10))
            f_k = jnp.where(is_j, -i01, jnp.where(is_k, -i11, cols[j] * i01 + cols[k] * i11))
            pivot = is_j | is_k

            def swept(v):
                return jnp.where(pivot, 0.0, v) - (f_j * spread(v, j) + f_k * spread(v, k))

            for m in range(j + 2, 8):
                cols[m] = swept(cols[m])
            panel = swept(panel)
        scaled.append(jnp.where(known, panel, 0.0))
        rows = [spread(panel, j) for j in range(8)]
        if work:
            work.pop(0)()
        for s in range(t + 1, count):
            v = tiles[s]
            p = [jnp.broadcast_to(v[:, q + j : q + j + 1], (8, width)) * rows[j] for j in range(8)]
            total = ((p[0] + p[1]) + (p[2] + p[3])) + ((p[4] + p[5]) + (p[6] + p[7]))
            tiles[s] = jnp.where(here, 0.0, v) - total
    return jnp.concatenate(lower, axis=0), jnp.concatenate(scaled, axis=0)


def invert(at_ref, own_ref, other_ref, out_ref, zero_ref):
    tiles, half, n = own_ref.shape
    low_is_own = at_ref[0] % 2 == 0
    for t in range(tiles):
        own, other = own_ref[t], other_ref[t]
        low, high = jnp.where(low_is_own, own, other), jnp.where(low_is_own, other, own)
        for j in range(n // BASE):
            lanes = slice(BASE * j, BASE * j + BASE)
            out_ref[j, pl.ds(t, half, stride=tiles), :] = low[:, lanes]
            out_ref[j, pl.ds(t + half * tiles, half, stride=tiles), :] = high[:, lanes]
    zero_ref[...] = jnp.zeros_like(zero_ref)
    zero = zero_ref[...]
    blocks = n // BASE
    work = []
    for k in range(blocks):
        own = slice(BASE * k, BASE * k + BASE)
        diagonal = out_ref[k, own, :]
        lower, scaled = base_factors([diagonal[s : s + 8] for s in range(0, BASE, 8)], zero, work)
        while work:
            work.pop(0)()
        base = across(lower, scaled, ((0,), (0,)), HIGH)
        rows = {k: base}
        cols = [out_ref[k, BASE * r : BASE * r + BASE, :] for r in range(blocks)]
        out_ref[k, own, :] = base

        def row(c, own=own, rows=rows, base=base):
            rows[c] = across(base, out_ref[c, own, :], ((1,), (0,)), HIGH)
            out_ref[c, own, :] = rows[c]

        def product(r, c, k=k, rows=rows, cols=cols):
            at = (c, slice(BASE * r, BASE * r + BASE))
            total = across(cols[r], rows[c], ((1,), (0,)), HIGH)
            out_ref[at] = -total if c == k else out_ref[at] - total

        following = (k + 1) % blocks
        if k + 1 < blocks:
            row(following)
            product(following, following)
        for c in [(k + i) % blocks for i in range(1, blocks)]:
            if c != following or k + 1 == blocks:
                work.append(functools.partial(row, c))
        for c in [(k + i) % blocks for i in range(1, blocks + 1)]:
            for r in [(k + i) % blocks for i in range(1, blocks)]:
                if not r == c == k + 1:
                    work.append(functools.partial(product, r, c))
    while work:
        work.pop(0)()


def update(at_ref, pruned_ref, inv_ref, near_ref, far_ref, twin_near_ref, twin_far_ref, *refs):
    blocks, (h_ref, w_ref, h_out, w_out, panel_ref, w_new_ref, h_new_ref, sems) = refs[:-8], refs[-8:]
    strips, n, _ = inv_ref.shape
    width = h_ref.shape[1]
    tiles = 4 * near_ref.shape[0]
    first = first_places(pruned_ref[...], tiles, h_ref.shape[0])
    cap = 2 * n // tiles
    side = len(blocks) // 2
    rows_w = w_ref.shape[1]
    steps = rows_w // BLOCK
    core, z = at_ref[0] % 2, at_ref[0] // 2
    near = near_ref.shape[0]
    for t in range(tiles):
        apart = (t // 2) ^ z
        of = apart % near
        own = jnp.where(apart < near, near_ref[of], far_ref[of])
        twin = jnp.where(apart < near, twin_near_ref[of], twin_far_ref[of])
        place_strips(panel_ref, first[t], jnp.where(core == t % 2, own, twin), cap, width)
    panel = jnp.concatenate([panel_ref[j, 0:n, :] for j in range(panel_ref.shape[0])], axis=1).T[:width, :]
    x, y = at_ref[1] % side, at_ref[1] // side
    hands = []
    for path in range(2):
        for far in range(side):
            for near in range(side):
                dx, dy = (near, far) if path == 0 else (far, near)
                hand = (y + side - dy) % side * side + (x + side - dx) % side
                hands.append(hand + path * (n // 2))
    inverse = jnp.concatenate(
        [
            jnp.concatenate([inv_ref[j, pl.ds(h, n // tiles // 2, stride=tiles), :] for h in hands], axis=0)
            for j in range(strips)
        ],
        axis=1,
    )
    solved = across(panel, inverse, ((1,), (1,)), HIGH)
    high = solved.astype(BF16)
    low = (solved - high.astype(F32)).astype(BF16)
    unit = lax.broadcasted_iota(jnp.int32, (width, n), 0) + at_ref[1] * width
    keep = 1.0 - jnp.sum(jnp.where(unit == pruned_ref[...], 1.0, 0.0), axis=1, keepdims=True)
    apply = ((1,), (0,))

    def cols(start, size):
        return jnp.concatenate([b[:, start : start + size] for b in blocks], axis=0)

    copies = []
    for i in range(steps):
        at = slice(BLOCK * i, BLOCK * i + BLOCK)
        got = cols(BLOCK * i, BLOCK)
        total = across(high, got, apply) + across(low, got, apply)
        w_new_ref[:, at] = (w_ref[:, at].astype(F32) - total) * keep
        copies.append(pltpu.make_async_copy(w_new_ref.at[:, at], w_out.at[:, at], sems.at[i]))
        copies[-1].start()
    c_high, c_low = cols(rows_w, width), cols(rows_w + lanes_for(width), width)
    total = across(high, c_high, apply) + (across(low, c_high, apply) + across(high, c_low, apply))
    h_new_ref[...] = h_ref[...] - total.T
    copies.append(pltpu.make_async_copy(h_new_ref, h_out, sems.at[steps]))
    copies[-1].start()
    for copy in copies:
        copy.wait()


def sent_to_all(copies, axis):
    return lax.all_to_all(copies, axis, split_axis=0, concat_axis=0, tiled=True)


def on_device(hessian_inverse, weights, pruned):
    tile_rows, tile_cols = hessian_inverse.shape
    rows_w = weights.shape[0]
    n = pruned.shape[0]
    tiles = lax.axis_size("row")
    cap = 2 * n // tiles
    at = jnp.stack([lax.axis_index("row"), lax.axis_index("col")]).astype(jnp.int32)
    weights = weights.T
    listed = pruned.reshape(1, n)
    length = rows_w + 2 * lanes_for(tile_rows)
    hands = pl.pallas_call(
        pack_cols,
        out_shape=jax.ShapeDtypeStruct((8 * tiles, length // 2), BF16),
        in_specs=[VMEM, ANY, ANY],
        out_specs=VMEM,
        scratch_shapes=[
            pltpu.VMEM(hessian_inverse.shape, F32),
            pltpu.VMEM(weights.shape, BF16),
            pltpu.SemaphoreType.DMA((3,)),
        ],
        name="pack_cols",
    )(listed, hessian_inverse, weights)
    hands = sent_to_all(hands, "col")
    mine = n // tiles
    rows = pl.pallas_call(
        pack_rows,
        out_shape=jax.ShapeDtypeStruct((cap * tile_cols // 128, 128), F32),
        in_specs=[SMEM, VMEM, VMEM],
        out_specs=VMEM,
        name="pack_rows",
    )(at, listed, hessian_inverse)

    def swapped(value, mask):
        return lax.ppermute(value, "row", [(i, i ^ mask) for i in range(tiles)])

    near_rows = [rows] + [swapped(rows, 2 * m) for m in range(1, 4)]
    near_rows = jnp.stack(near_rows)
    low, high, pieces = pl.pallas_call(
        functools.partial(gather_hand, height=tile_rows, width=tile_cols),
        out_shape=(
            jax.ShapeDtypeStruct((mine // 2, length), BF16),
            jax.ShapeDtypeStruct((mine // 2, length), BF16),
            jax.ShapeDtypeStruct((tiles, 8, cap // 8 * (mine // 2)), F32),
        ),
        in_specs=[SMEM, VMEM, ANY],
        out_specs=(VMEM, VMEM, VMEM),
        scratch_shapes=[pltpu.VMEM(hands.shape, BF16), pltpu.SemaphoreType.DMA(())],
        name="gather_hand",
    )(at, listed, hands)
    pieces = sent_to_all(pieces, "row")
    side = math.isqrt(tiles)

    def along_x(value, d):
        return lax.ppermute(value, "col", [(c, c // side * side + (c + d) % side) for c in range(tiles)])

    def along_y(value, d):
        return lax.ppermute(value, "col", [(c, (c + d * side) % tiles) for c in range(tiles)])

    lows = [low] + [along_x(low, d) for d in range(1, side)]
    highs = [high] + [along_y(high, d) for d in range(1, side)]
    slab = pl.pallas_call(
        functools.partial(pack_slab, width=tile_rows),
        out_shape=jax.ShapeDtypeStruct((tiles, mine // 2, n), F32),
        in_specs=[VMEM, VMEM],
        out_specs=VMEM,
        scratch_shapes=[pltpu.VMEM((n + cap, 128), F32)],
        name="pack_slab",
    )(listed, pieces)
    slab = sent_to_all(slab, "col")
    low, high = pl.pallas_call(
        join,
        out_shape=(jax.ShapeDtypeStruct((side * mine // 2, length), BF16),) * 2,
        in_specs=[ANY] * (2 * side),
        out_specs=(ANY, ANY),
        scratch_shapes=[pltpu.SemaphoreType.DMA((2 * side,))],
        name="join",
    )(*lows, *highs)
    cols = [low] + [along_y(low, d) for d in range(1, side)]
    cols += [high] + [along_x(high, d) for d in range(1, side)]
    far_rows = swapped(near_rows, 8)
    twin_near = swapped(near_rows, 1)
    slab_twin = swapped(slab, 1)
    inverse = pl.pallas_call(
        invert,
        out_shape=jax.ShapeDtypeStruct((n // BASE, n, BASE), F32),
        in_specs=[SMEM, VMEM, VMEM],
        out_specs=VMEM,
        scratch_shapes=[pltpu.VMEM((8, BASE), F32)],
        name="invert",
    )(at, slab, slab_twin)
    twin_far = swapped(far_rows, 1)
    h_new, w_new = pl.pallas_call(
        update,
        out_shape=(
            jax.ShapeDtypeStruct(hessian_inverse.shape, F32),
            jax.ShapeDtypeStruct(weights.shape, F32),
        ),
        in_specs=[SMEM] + [VMEM] * (8 + len(cols)),
        out_specs=(ANY, ANY),
        scratch_shapes=[
            pltpu.VMEM((-(-tile_cols // 128), n + cap, 128), F32),
            pltpu.VMEM(weights.shape, F32),
            pltpu.VMEM(hessian_inverse.shape, F32),
            pltpu.SemaphoreType.DMA((rows_w // BLOCK + 1,)),
        ],
        name="update",
    )(
        at, listed, inverse, near_rows, far_rows, twin_near, twin_far, *cols, hessian_inverse, weights
    )
    return h_new, w_new.T


def solution(mesh):
    specs = (P("row", "col"), P("row", "col"))

    return jax.shard_map(on_device, mesh=mesh, in_specs=(*specs, P()), out_specs=specs, check_vma=False)
```

```python
import functools
import math

import jax
import jax.numpy as jnp
from jax import lax
from jax.experimental import pallas as pl
from jax.experimental.pallas import tpu as pltpu
from jax.sharding import PartitionSpec as P


HIGH = lax.Precision.HIGHEST
F32 = jnp.float32
BF16 = jnp.bfloat16
VMEM = pl.BlockSpec(memory_space=pltpu.VMEM)
SMEM = pl.BlockSpec(memory_space=pltpu.SMEM)
ANY = pl.BlockSpec(memory_space=pl.ANY)
BASE = 128
BLOCK = 256


def across(a, b, dims, precision=None):
    return lax.dot_general(a, b, (dims, ((), ())), precision=precision, preferred_element_type=F32)


def one_hot(index, width):
    slots = index.shape[0]
    return jnp.where(index == lax.broadcasted_iota(jnp.int32, (slots, width), 1), 1.0, 0.0)


def held(pruned, tile, width, place):
    low = tile * width
    before = jnp.sum(jnp.where(pruned < low, 1, 0), axis=1, keepdims=True)
    place = place(before)
    lane = lax.broadcasted_iota(jnp.int32, (place.shape[0], pruned.shape[1]), 1)
    here = (lane == place) & (pruned >= low) & (pruned < low + width)
    return jnp.sum(jnp.where(here, pruned - low + 1, 0), axis=1, keepdims=True) - 1


def in_turn(cap):
    slot = lax.broadcasted_iota(jnp.int32, (cap, 1), 0)
    return lambda before: before + slot


def dealt(before, tiles, slots):
    slot = lax.broadcasted_iota(jnp.int32, (tiles * 2 * slots, 1), 0)
    hand, second, turn = slot // (2 * slots), slot // slots % 2, slot % slots
    return hand, second, (before - hand + tiles - 1) // tiles + turn


def lanes_for(width):
    return -(-width // 128) * 128


def pack_rows(at_ref, pruned_ref, h_ref, rows_ref):
    height, width = h_ref.shape
    cap = rows_ref.shape[0] * 128 // width
    pick = one_hot(held(pruned_ref[...], at_ref[0], height, in_turn(cap)), height)
    rows_ref[...] = strips_of(across(pick, h_ref[...], ((1,), (0,)), HIGH))


def strips_of(rows):
    count, width = rows.shape
    full = width // 128 * 128
    rest = width - full
    groups = 128 // rest
    each = count // groups
    strips = [rows[:, j : j + 128] for j in range(0, full, 128)]
    strips.append(jnp.concatenate([rows[each * i : each * i + each, full:] for i in range(groups)], axis=1))
    return jnp.concatenate(strips, axis=0)


def place_strips(ref, start, packed, count, width):
    full = width // 128
    rest = width - 128 * full
    each = count * rest // 128
    for j in range(full):
        ref[j, pl.ds(start, count), :] = packed[count * j : count * j + count]
    last = packed[count * full :]
    for i in range(128 // rest):
        ref[full, pl.ds(start + each * i, each), 0:rest] = last[:, rest * i : rest * i + rest]


def pack_cols(pruned_ref, h_hbm, w_hbm, out_ref, h_ref, w_ref, sems):
    slots, half = out_ref.shape
    copies = [
        pltpu.make_async_copy(h_hbm, h_ref, sems.at[0]),
        pltpu.make_async_copy(w_hbm.at[:, half:], w_ref.at[:, half:], sems.at[1]),
        pltpu.make_async_copy(w_hbm.at[:, :half], w_ref.at[:, :half], sems.at[2]),
    ]
    for copy in copies:
        copy.start()
    pruned = pruned_ref[...]
    width = h_ref.shape[1]
    tiles = slots // 8
    pick = one_hot(held(pruned, lax.axis_index("col"), width, lambda before: dealt_places(before, tiles, 4)), width)
    picked = pick.astype(BF16)
    copies[0].wait()
    c = across(pick, h_ref[...], ((1,), (1,)), HIGH)
    c_high = c.astype(BF16).astype(F32)
    copies[1].wait()
    last = across(picked, w_ref[:, half:], ((1,), (0,)))
    spare = jnp.zeros((slots, lanes_for(width) - width), F32)
    last = jnp.concatenate([last, c_high, spare, c - c_high, spare], axis=1)
    second = lax.broadcasted_iota(jnp.int32, (slots, 1), 0) // 4 % 2
    copies[2].wait()
    first = across(picked, w_ref[:, :half], ((1,), (0,)))
    out_ref[...] = jnp.where(second == 1, last, first).astype(BF16)


def dealt_places(before, tiles, slots):
    hand, _, turn = dealt(before, tiles, slots)
    return hand + tiles * turn


def gather_hand(at_ref, pruned_ref, got_ref, low_ref, high_ref, piece_ref, *, height, width):
    pruned = pruned_ref[...]
    slots, half = got_ref.shape
    tiles = piece_ref.shape[0]
    mine = pruned.shape[1] // tiles
    slot = lax.broadcasted_iota(jnp.int32, (slots, 1), 0)
    tile, second, turn = slot // 8, slot // 4 % 2, slot % 4
    before = jnp.sum(jnp.where(pruned < tile * width, 1, 0), axis=1, keepdims=True)
    after = jnp.sum(jnp.where(pruned < tile * width + width, 1, 0), axis=1, keepdims=True)
    hand = at_ref[1]
    turn = (before - hand + tiles - 1) // tiles + turn
    turn = jnp.where(hand + tiles * turn < after, turn, -1)
    got = got_ref[...]
    parts = [
        across(one_hot(jnp.where(second == part, turn, -1), mine).astype(BF16), got, ((0,), (0,)))
        for part in range(2)
    ]
    wide = lanes_for(height)
    c = parts[1][:, half - 2 * wide : half - 2 * wide + height] + parts[1][:, half - wide : half - wide + height]
    cap = 2 * mine
    pick = one_hot(held(pruned, at_ref[0], height, in_turn(cap)), height)
    piece = across(pick, c, ((1,), (1,)), HIGH)
    for core in range(2):
        part = piece[:, mine // 2 * core : mine // 2 * (core + 1)]
        part = jnp.concatenate([part[8 * i : 8 * i + 8] for i in range(cap // 8)], axis=1)
        for d in range(core, tiles, 2):
            piece_ref[d] = part
    for part in range(2):
        lanes = slice(half * part, half * part + half)
        low_ref[:, lanes] = parts[part][: mine // 2].astype(BF16)
        high_ref[:, lanes] = parts[part][mine // 2 :].astype(BF16)


def join(*refs):
    count = (len(refs) - 2) // 2
    for path in range(2):
        out = refs[2 * count + path]
        rows = out.shape[0] // count
        for d in range(count):
            out[rows * d : rows * d + rows, :] = refs[count * path + d][...]


def pack_slab(pruned_ref, got_ref, out_ref, slab_ref, *, width):
    tiles, mine, n = out_ref.shape
    groups = got_ref.shape[2] // mine
    first = first_places(pruned_ref[...], tiles, width)
    for t in range(tiles):
        got = got_ref[t]
        for i in range(groups):
            slab_ref[pl.ds(first[t] + 8 * i, 8), 0:mine] = got[:, mine * i : mine * i + mine]
    slab = slab_ref[0:n, :].T[0:mine, :]
    for d in range(tiles):
        out_ref[d] = slab


def first_places(pruned, tiles, width):
    return [jnp.sum(jnp.where(pruned < t * width, 1, 0)) for t in range(tiles)]


def spread(v, i):
    return jnp.broadcast_to(v[i : i + 1, :], v.shape)


def base_factors(tiles, zero, work):
    width = tiles[0].shape[1]
    lane = lax.broadcasted_iota(jnp.int32, (8, width), 1)
    sub = lax.broadcasted_iota(jnp.int32, (8, width), 0)
    tiles = list(tiles)
    count = len(tiles)
    lower, scaled = [], []
    for t in range(count):
        q = 8 * t
        own = tiles[t]
        cols = [jnp.broadcast_to(own[:, q + j : q + j + 1], (8, width)) + zero for j in range(8)]
        here = (lane >= q) & (lane < q + 8)
        known = lane < q + 8
        panel = jnp.where(here, jnp.where(lane - q == sub, 1.0, 0.0), own)
        lower.append(jnp.where(known, panel, 0.0))
        for j in range(0, 8, 2):
            k = j + 1
            a, b, b2, c = spread(cols[j], j), spread(cols[k], j), spread(cols[j], k), spread(cols[k], k)
            r = 1.0 / (a * c - b * b2)
            i00, i01, i10, i11 = c * r, -(b * r), -(b2 * r), a * r
            is_j, is_k = sub == j, sub == k
            f_j = jnp.where(is_j, -i00, jnp.where(is_k, -i10, cols[j] * i00 + cols[k] * i10))
            f_k = jnp.where(is_j, -i01, jnp.where(is_k, -i11, cols[j] * i01 + cols[k] * i11))
            pivot = is_j | is_k

            def swept(v):
                return jnp.where(pivot, 0.0, v) - (f_j * spread(v, j) + f_k * spread(v, k))

            for m in range(j + 2, 8):
                cols[m] = swept(cols[m])
            panel = swept(panel)
        scaled.append(jnp.where(known, panel, 0.0))
        rows = [spread(panel, j) for j in range(8)]
        if work:
            work.pop(0)()
        for s in range(t + 1, count):
            v = tiles[s]
            p = [jnp.broadcast_to(v[:, q + j : q + j + 1], (8, width)) * rows[j] for j in range(8)]
            total = ((p[0] + p[1]) + (p[2] + p[3])) + ((p[4] + p[5]) + (p[6] + p[7]))
            tiles[s] = jnp.where(here, 0.0, v) - total
    return jnp.concatenate(lower, axis=0), jnp.concatenate(scaled, axis=0)


def invert(at_ref, own_ref, other_ref, out_ref, zero_ref):
    tiles, half, n = own_ref.shape
    low_is_own = at_ref[0] % 2 == 0
    for t in range(tiles):
        own, other = own_ref[t], other_ref[t]
        low, high = jnp.where(low_is_own, own, other), jnp.where(low_is_own, other, own)
        for j in range(n // BASE):
            lanes = slice(BASE * j, BASE * j + BASE)
            out_ref[j, pl.ds(t, half, stride=tiles), :] = low[:, lanes]
            out_ref[j, pl.ds(t + half * tiles, half, stride=tiles), :] = high[:, lanes]
    zero_ref[...] = jnp.zeros_like(zero_ref)
    zero = zero_ref[...]
    blocks = n // BASE
    work = []
    for k in range(blocks):
        own = slice(BASE * k, BASE * k + BASE)
        diagonal = out_ref[k, own, :]
        lower, scaled = base_factors([diagonal[s : s + 8] for s in range(0, BASE, 8)], zero, work)
        while work:
            work.pop(0)()
        base = across(lower, scaled, ((0,), (0,)), HIGH)
        rows = {k: base}
        cols = [out_ref[k, BASE * r : BASE * r + BASE, :] for r in range(blocks)]
        out_ref[k, own, :] = base

        def row(c, own=own, rows=rows, base=base):
            rows[c] = across(base, out_ref[c, own, :], ((1,), (0,)), HIGH)
            out_ref[c, own, :] = rows[c]

        def product(r, c, k=k, rows=rows, cols=cols):
            at = (c, slice(BASE * r, BASE * r + BASE))
            total = across(cols[r], rows[c], ((1,), (0,)), HIGH)
            out_ref[at] = -total if c == k else out_ref[at] - total

        following = (k + 1) % blocks
        if k + 1 < blocks:
            row(following)
            product(following, following)
        for c in [(k + i) % blocks for i in range(1, blocks)]:
            if c != following or k + 1 == blocks:
                work.append(functools.partial(row, c))
        for c in [(k + i) % blocks for i in range(1, blocks + 1)]:
            for r in [(k + i) % blocks for i in range(1, blocks)]:
                if not r == c == k + 1:
                    work.append(functools.partial(product, r, c))
    while work:
        work.pop(0)()


def update(at_ref, pruned_ref, inv_ref, near_ref, far_ref, twin_near_ref, twin_far_ref, *refs):
    blocks, (h_ref, w_ref, h_out, w_out, panel_ref, w_new_ref, h_new_ref, sems) = refs[:-8], refs[-8:]
    strips, n, _ = inv_ref.shape
    width = h_ref.shape[1]
    tiles = 4 * near_ref.shape[0]
    first = first_places(pruned_ref[...], tiles, h_ref.shape[0])
    cap = 2 * n // tiles
    side = len(blocks) // 2
    rows_w = w_ref.shape[1]
    steps = rows_w // BLOCK
    core, z = at_ref[0] % 2, at_ref[0] // 2
    near = near_ref.shape[0]
    for t in range(tiles):
        apart = (t // 2) ^ z
        of = apart % near
        own = jnp.where(apart < near, near_ref[of], far_ref[of])
        twin = jnp.where(apart < near, twin_near_ref[of], twin_far_ref[of])
        place_strips(panel_ref, first[t], jnp.where(core == t % 2, own, twin), cap, width)
    panel = jnp.concatenate([panel_ref[j, 0:n, :] for j in range(panel_ref.shape[0])], axis=1).T[:width, :]
    x, y = at_ref[1] % side, at_ref[1] // side
    hands = []
    for path in range(2):
        for far in range(side):
            for near in range(side):
                dx, dy = (near, far) if path == 0 else (far, near)
                hand = (y + side - dy) % side * side + (x + side - dx) % side
                hands.append(hand + path * (n // 2))
    inverse = jnp.concatenate(
        [
            jnp.concatenate([inv_ref[j, pl.ds(h, n // tiles // 2, stride=tiles), :] for h in hands], axis=0)
            for j in range(strips)
        ],
        axis=1,
    )
    solved = across(panel, inverse, ((1,), (1,)), HIGH)
    high = solved.astype(BF16)
    low = (solved - high.astype(F32)).astype(BF16)
    unit = lax.broadcasted_iota(jnp.int32, (width, n), 0) + at_ref[1] * width
    keep = 1.0 - jnp.sum(jnp.where(unit == pruned_ref[...], 1.0, 0.0), axis=1, keepdims=True)
    apply = ((1,), (0,))

    def cols(start, size):
        return jnp.concatenate([b[:, start : start + size] for b in blocks], axis=0)

    copies = []
    for i in range(steps):
        at = slice(BLOCK * i, BLOCK * i + BLOCK)
        got = cols(BLOCK * i, BLOCK)
        total = across(high, got, apply) + across(low, got, apply)
        w_new_ref[:, at] = (w_ref[:, at].astype(F32) - total) * keep
        copies.append(pltpu.make_async_copy(w_new_ref.at[:, at], w_out.at[:, at], sems.at[i]))
        copies[-1].start()
    c_high, c_low = cols(rows_w, width), cols(rows_w + lanes_for(width), width)
    total = across(high, c_high, apply) + (across(low, c_high, apply) + across(high, c_low, apply))
    h_new_ref[...] = h_ref[...] - total.T
    copies.append(pltpu.make_async_copy(h_new_ref, h_out, sems.at[steps]))
    copies[-1].start()
    for copy in copies:
        copy.wait()


def sent_to_all(copies, axis):
    return lax.all_to_all(copies, axis, split_axis=0, concat_axis=0, tiled=True)


def on_device(hessian_inverse, weights, pruned):
    tile_rows, tile_cols = hessian_inverse.shape
    rows_w = weights.shape[0]
    n = pruned.shape[0]
    tiles = lax.axis_size("row")
    cap = 2 * n // tiles
    at = jnp.stack([lax.axis_index("row"), lax.axis_index("col")]).astype(jnp.int32)
    weights = weights.T
    listed = pruned.reshape(1, n)
    length = rows_w + 2 * lanes_for(tile_rows)
    hands = pl.pallas_call(
        pack_cols,
        out_shape=jax.ShapeDtypeStruct((8 * tiles, length // 2), BF16),
        in_specs=[VMEM, ANY, ANY],
        out_specs=VMEM,
        scratch_shapes=[
            pltpu.VMEM(hessian_inverse.shape, F32),
            pltpu.VMEM(weights.shape, BF16),
            pltpu.SemaphoreType.DMA((3,)),
        ],
        name="pack_cols",
    )(listed, hessian_inverse, weights)
    hands = sent_to_all(hands, "col")
    mine = n // tiles
    rows = pl.pallas_call(
        pack_rows,
        out_shape=jax.ShapeDtypeStruct((cap * tile_cols // 128, 128), F32),
        in_specs=[SMEM, VMEM, VMEM],
        out_specs=VMEM,
        name="pack_rows",
    )(at, listed, hessian_inverse)

    def swapped(value, mask):
        return lax.ppermute(value, "row", [(i, i ^ mask) for i in range(tiles)])

    near_rows = [rows] + [swapped(rows, 2 * m) for m in range(1, 4)]
    near_rows = jnp.stack(near_rows)
    low, high, pieces = pl.pallas_call(
        functools.partial(gather_hand, height=tile_rows, width=tile_cols),
        out_shape=(
            jax.ShapeDtypeStruct((mine // 2, length), BF16),
            jax.ShapeDtypeStruct((mine // 2, length), BF16),
            jax.ShapeDtypeStruct((tiles, 8, cap // 8 * (mine // 2)), F32),
        ),
        in_specs=[SMEM, VMEM, VMEM],
        out_specs=(VMEM, VMEM, VMEM),
        name="gather_hand",
    )(at, listed, hands)
    pieces = sent_to_all(pieces, "row")
    side = math.isqrt(tiles)

    def along_x(value, d):
        return lax.ppermute(value, "col", [(c, c // side * side + (c + d) % side) for c in range(tiles)])

    def along_y(value, d):
        return lax.ppermute(value, "col", [(c, (c + d * side) % tiles) for c in range(tiles)])

    lows = [low] + [along_x(low, d) for d in range(1, side)]
    highs = [high] + [along_y(high, d) for d in range(1, side)]
    slab = pl.pallas_call(
        functools.partial(pack_slab, width=tile_rows),
        out_shape=jax.ShapeDtypeStruct((tiles, mine // 2, n), F32),
        in_specs=[VMEM, VMEM],
        out_specs=VMEM,
        scratch_shapes=[pltpu.VMEM((n + cap, 128), F32)],
        name="pack_slab",
    )(listed, pieces)
    slab = sent_to_all(slab, "col")
    low, high = pl.pallas_call(
        join,
        out_shape=(jax.ShapeDtypeStruct((side * mine // 2, length), BF16),) * 2,
        in_specs=[VMEM] * (2 * side),
        out_specs=(VMEM, VMEM),
        name="join",
    )(*lows, *highs)
    cols = [low] + [along_y(low, d) for d in range(1, side)]
    cols += [high] + [along_x(high, d) for d in range(1, side)]
    far_rows = swapped(near_rows, 8)
    twin_near = swapped(near_rows, 1)
    slab_twin = swapped(slab, 1)
    inverse = pl.pallas_call(
        invert,
        out_shape=jax.ShapeDtypeStruct((n // BASE, n, BASE), F32),
        in_specs=[SMEM, VMEM, VMEM],
        out_specs=VMEM,
        scratch_shapes=[pltpu.VMEM((8, BASE), F32)],
        name="invert",
    )(at, slab, slab_twin)
    twin_far = swapped(far_rows, 1)
    h_new, w_new = pl.pallas_call(
        update,
        out_shape=(
            jax.ShapeDtypeStruct(hessian_inverse.shape, F32),
            jax.ShapeDtypeStruct(weights.shape, F32),
        ),
        in_specs=[SMEM] + [VMEM] * (8 + len(cols)),
        out_specs=(ANY, ANY),
        scratch_shapes=[
            pltpu.VMEM((-(-tile_cols // 128), n + cap, 128), F32),
            pltpu.VMEM(weights.shape, F32),
            pltpu.VMEM(hessian_inverse.shape, F32),
            pltpu.SemaphoreType.DMA((rows_w // BLOCK + 1,)),
        ],
        name="update",
    )(
        at, listed, inverse, near_rows, far_rows, twin_near, twin_far, *cols, hessian_inverse, weights
    )
    return h_new, w_new.T


def solution(mesh):
    specs = (P("row", "col"), P("row", "col"))

    return jax.shard_map(on_device, mesh=mesh, in_specs=(*specs, P()), out_specs=specs, check_vma=False)
```

```python
import functools
import math

import jax
import jax.numpy as jnp
from jax import lax
from jax.experimental import pallas as pl
from jax.experimental.pallas import tpu as pltpu
from jax.sharding import PartitionSpec as P


HIGH = lax.Precision.HIGHEST
F32 = jnp.float32
BF16 = jnp.bfloat16
VMEM = pl.BlockSpec(memory_space=pltpu.VMEM)
SMEM = pl.BlockSpec(memory_space=pltpu.SMEM)
ANY = pl.BlockSpec(memory_space=pl.ANY)
BASE = 128
GRANT = 24 << 20
BLOCK = 256


def across(a, b, dims, precision=None):
    return lax.dot_general(a, b, (dims, ((), ())), precision=precision, preferred_element_type=F32)


def one_hot(index, width):
    slots = index.shape[0]
    return jnp.where(index == lax.broadcasted_iota(jnp.int32, (slots, width), 1), 1.0, 0.0)


def held(pruned, tile, width, place):
    low = tile * width
    before = jnp.sum(jnp.where(pruned < low, 1, 0), axis=1, keepdims=True)
    place = place(before)
    lane = lax.broadcasted_iota(jnp.int32, (place.shape[0], pruned.shape[1]), 1)
    here = (lane == place) & (pruned >= low) & (pruned < low + width)
    return jnp.sum(jnp.where(here, pruned - low + 1, 0), axis=1, keepdims=True) - 1


def in_turn(cap):
    slot = lax.broadcasted_iota(jnp.int32, (cap, 1), 0)
    return lambda before: before + slot


def dealt(before, tiles, slots):
    slot = lax.broadcasted_iota(jnp.int32, (tiles * 2 * slots, 1), 0)
    hand, second, turn = slot // (2 * slots), slot // slots % 2, slot % slots
    return hand, second, (before - hand + tiles - 1) // tiles + turn


def lanes_for(width):
    return -(-width // 128) * 128


def pack_rows(at_ref, pruned_ref, h_ref, rows_ref):
    height, width = h_ref.shape
    cap = rows_ref.shape[0] * 128 // width
    pick = one_hot(held(pruned_ref[...], at_ref[0], height, in_turn(cap)), height)
    rows_ref[...] = strips_of(across(pick, h_ref[...], ((1,), (0,)), HIGH))


def strips_of(rows):
    count, width = rows.shape
    full = width // 128 * 128
    rest = width - full
    groups = 128 // rest
    each = count // groups
    strips = [rows[:, j : j + 128] for j in range(0, full, 128)]
    strips.append(jnp.concatenate([rows[each * i : each * i + each, full:] for i in range(groups)], axis=1))
    return jnp.concatenate(strips, axis=0)


def place_strips(ref, start, packed, count, width):
    full = width // 128
    rest = width - 128 * full
    each = count * rest // 128
    for j in range(full):
        ref[j, pl.ds(start, count), :] = packed[count * j : count * j + count]
    last = packed[count * full :]
    for i in range(128 // rest):
        ref[full, pl.ds(start + each * i, each), 0:rest] = last[:, rest * i : rest * i + rest]


def pack_cols(pruned_ref, h_ref, w_ref, out_ref):
    pruned = pruned_ref[...]
    slots, half = out_ref.shape
    width = h_ref.shape[1]
    tiles = slots // 8
    pick = one_hot(held(pruned, lax.axis_index("col"), width, lambda before: dealt_places(before, tiles, 4)), width)
    w = w_ref[...]
    picked = pick.astype(BF16)
    first = across(picked, w[:, :half], ((1,), (0,)))
    last = across(picked, w[:, half:], ((1,), (0,)))
    c = across(pick, h_ref[...], ((1,), (1,)), HIGH)
    c_high = c.astype(BF16).astype(F32)
    spare = jnp.zeros((slots, lanes_for(width) - width), F32)
    last = jnp.concatenate([last, c_high, spare, c - c_high, spare], axis=1)
    second = lax.broadcasted_iota(jnp.int32, (slots, 1), 0) // 4 % 2
    out_ref[...] = jnp.where(second == 1, last, first).astype(BF16)


def dealt_places(before, tiles, slots):
    hand, _, turn = dealt(before, tiles, slots)
    return hand + tiles * turn


def gather_hand(at_ref, pruned_ref, got_ref, low_ref, high_ref, piece_ref, *, height, width):
    pruned = pruned_ref[...]
    slots, half = got_ref.shape
    tiles = piece_ref.shape[0]
    mine = pruned.shape[1] // tiles
    slot = lax.broadcasted_iota(jnp.int32, (slots, 1), 0)
    tile, second, turn = slot // 8, slot // 4 % 2, slot % 4
    before = jnp.sum(jnp.where(pruned < tile * width, 1, 0), axis=1, keepdims=True)
    after = jnp.sum(jnp.where(pruned < tile * width + width, 1, 0), axis=1, keepdims=True)
    hand = at_ref[1]
    turn = (before - hand + tiles - 1) // tiles + turn
    turn = jnp.where(hand + tiles * turn < after, turn, -1)
    got = got_ref[...]
    parts = [
        across(one_hot(jnp.where(second == part, turn, -1), mine).astype(BF16), got, ((0,), (0,)))
        for part in range(2)
    ]
    wide = lanes_for(height)
    c = parts[1][:, half - 2 * wide : half - 2 * wide + height] + parts[1][:, half - wide : half - wide + height]
    cap = 2 * mine
    pick = one_hot(held(pruned, at_ref[0], height, in_turn(cap)), height)
    piece = across(pick, c, ((1,), (1,)), HIGH)
    for core in range(2):
        part = piece[:, mine // 2 * core : mine // 2 * (core + 1)]
        part = jnp.concatenate([part[8 * i : 8 * i + 8] for i in range(cap // 8)], axis=1)
        for d in range(core, tiles, 2):
            piece_ref[d] = part
    for part in range(2):
        lanes = slice(half * part, half * part + half)
        low_ref[:, lanes] = parts[part][: mine // 2].astype(BF16)
        high_ref[:, lanes] = parts[part][mine // 2 :].astype(BF16)


def join(*refs):
    count = (len(refs) - 2) // 2
    for path in range(2):
        out = refs[2 * count + path]
        rows = out.shape[0] // count
        for d in range(count):
            out[rows * d : rows * d + rows, :] = refs[count * path + d][...]


def pack_slab(pruned_ref, got_ref, out_ref, slab_ref, *, width):
    tiles, mine, n = out_ref.shape
    groups = got_ref.shape[2] // mine
    first = first_places(pruned_ref[...], tiles, width)
    for t in range(tiles):
        got = got_ref[t]
        for i in range(groups):
            slab_ref[pl.ds(first[t] + 8 * i, 8), 0:mine] = got[:, mine * i : mine * i + mine]
    slab = slab_ref[0:n, :].T[0:mine, :]
    for d in range(tiles):
        out_ref[d] = slab


def first_places(pruned, tiles, width):
    return [jnp.sum(jnp.where(pruned < t * width, 1, 0)) for t in range(tiles)]


def spread(v, i):
    return jnp.broadcast_to(v[i : i + 1, :], v.shape)


def base_factors(tiles, zero, work):
    width = tiles[0].shape[1]
    lane = lax.broadcasted_iota(jnp.int32, (8, width), 1)
    sub = lax.broadcasted_iota(jnp.int32, (8, width), 0)
    tiles = list(tiles)
    count = len(tiles)
    lower, scaled = [], []
    for t in range(count):
        q = 8 * t
        own = tiles[t]
        cols = [jnp.broadcast_to(own[:, q + j : q + j + 1], (8, width)) + zero for j in range(8)]
        here = (lane >= q) & (lane < q + 8)
        known = lane < q + 8
        panel = jnp.where(here, jnp.where(lane - q == sub, 1.0, 0.0), own)
        lower.append(jnp.where(known, panel, 0.0))
        for j in range(0, 8, 2):
            k = j + 1
            a, b, b2, c = spread(cols[j], j), spread(cols[k], j), spread(cols[j], k), spread(cols[k], k)
            r = 1.0 / (a * c - b * b2)
            i00, i01, i10, i11 = c * r, -(b * r), -(b2 * r), a * r
            is_j, is_k = sub == j, sub == k
            f_j = jnp.where(is_j, -i00, jnp.where(is_k, -i10, cols[j] * i00 + cols[k] * i10))
            f_k = jnp.where(is_j, -i01, jnp.where(is_k, -i11, cols[j] * i01 + cols[k] * i11))
            pivot = is_j | is_k

            def swept(v):
                return jnp.where(pivot, 0.0, v) - (f_j * spread(v, j) + f_k * spread(v, k))

            for m in range(j + 2, 8):
                cols[m] = swept(cols[m])
            panel = swept(panel)
        scaled.append(jnp.where(known, panel, 0.0))
        rows = [spread(panel, j) for j in range(8)]
        if work:
            work.pop(0)()
        for s in range(t + 1, count):
            v = tiles[s]
            p = [jnp.broadcast_to(v[:, q + j : q + j + 1], (8, width)) * rows[j] for j in range(8)]
            total = ((p[0] + p[1]) + (p[2] + p[3])) + ((p[4] + p[5]) + (p[6] + p[7]))
            tiles[s] = jnp.where(here, 0.0, v) - total
    return jnp.concatenate(lower, axis=0), jnp.concatenate(scaled, axis=0)


def invert(at_ref, own_ref, other_ref, out_ref, zero_ref):
    tiles, half, n = own_ref.shape
    low_is_own = at_ref[0] % 2 == 0
    for t in range(tiles):
        own, other = own_ref[t], other_ref[t]
        low, high = jnp.where(low_is_own, own, other), jnp.where(low_is_own, other, own)
        for j in range(n // BASE):
            lanes = slice(BASE * j, BASE * j + BASE)
            out_ref[j, pl.ds(t, half, stride=tiles), :] = low[:, lanes]
            out_ref[j, pl.ds(t + half * tiles, half, stride=tiles), :] = high[:, lanes]
    zero_ref[...] = jnp.zeros_like(zero_ref)
    zero = zero_ref[...]
    blocks = n // BASE
    work = []
    for k in range(blocks):
        own = slice(BASE * k, BASE * k + BASE)
        diagonal = out_ref[k, own, :]
        lower, scaled = base_factors([diagonal[s : s + 8] for s in range(0, BASE, 8)], zero, work)
        while work:
            work.pop(0)()
        base = across(lower, scaled, ((0,), (0,)), HIGH)
        rows = {k: base}
        cols = [out_ref[k, BASE * r : BASE * r + BASE, :] for r in range(blocks)]
        out_ref[k, own, :] = base

        def row(c, own=own, rows=rows, base=base):
            rows[c] = across(base, out_ref[c, own, :], ((1,), (0,)), HIGH)
            out_ref[c, own, :] = rows[c]

        def product(r, c, k=k, rows=rows, cols=cols):
            at = (c, slice(BASE * r, BASE * r + BASE))
            total = across(cols[r], rows[c], ((1,), (0,)), HIGH)
            out_ref[at] = -total if c == k else out_ref[at] - total

        following = (k + 1) % blocks
        if k + 1 < blocks:
            row(following)
            product(following, following)
        for c in [(k + i) % blocks for i in range(1, blocks)]:
            if c != following or k + 1 == blocks:
                work.append(functools.partial(row, c))
        for c in [(k + i) % blocks for i in range(1, blocks + 1)]:
            for r in [(k + i) % blocks for i in range(1, blocks)]:
                if not r == c == k + 1:
                    work.append(functools.partial(product, r, c))
    while work:
        work.pop(0)()


def update(at_ref, pruned_ref, inv_ref, near_ref, far_ref, twin_near_ref, twin_far_ref, *refs):
    blocks, (h_ref, w_ref, h_out, w_out, panel_ref, w_new_ref, h_new_ref, sems) = refs[:-8], refs[-8:]
    strips, n, _ = inv_ref.shape
    width = h_ref.shape[1]
    tiles = 4 * near_ref.shape[0]
    first = first_places(pruned_ref[...], tiles, h_ref.shape[0])
    cap = 2 * n // tiles
    side = len(blocks) // 2
    rows_w = w_ref.shape[1]
    steps = rows_w // BLOCK
    core, z = at_ref[0] % 2, at_ref[0] // 2
    near = near_ref.shape[0]
    for t in range(tiles):
        apart = (t // 2) ^ z
        of = apart % near
        own = jnp.where(apart < near, near_ref[of], far_ref[of])
        twin = jnp.where(apart < near, twin_near_ref[of], twin_far_ref[of])
        place_strips(panel_ref, first[t], jnp.where(core == t % 2, own, twin), cap, width)
    panel = jnp.concatenate([panel_ref[j, 0:n, :] for j in range(panel_ref.shape[0])], axis=1).T[:width, :]
    x, y = at_ref[1] % side, at_ref[1] // side
    hands = []
    for path in range(2):
        for far in range(side):
            for near in range(side):
                dx, dy = (near, far) if path == 0 else (far, near)
                hand = (y + side - dy) % side * side + (x + side - dx) % side
                hands.append(hand + path * (n // 2))
    inverse = jnp.concatenate(
        [
            jnp.concatenate([inv_ref[j, pl.ds(h, n // tiles // 2, stride=tiles), :] for h in hands], axis=0)
            for j in range(strips)
        ],
        axis=1,
    )
    solved = across(panel, inverse, ((1,), (1,)), HIGH)
    high = solved.astype(BF16)
    low = (solved - high.astype(F32)).astype(BF16)
    unit = lax.broadcasted_iota(jnp.int32, (width, n), 0) + at_ref[1] * width
    keep = 1.0 - jnp.sum(jnp.where(unit == pruned_ref[...], 1.0, 0.0), axis=1, keepdims=True)
    apply = ((1,), (0,))

    def cols(start, size):
        return jnp.concatenate([b[:, start : start + size] for b in blocks], axis=0)

    copies = []
    for i in range(steps):
        at = slice(BLOCK * i, BLOCK * i + BLOCK)
        got = cols(BLOCK * i, BLOCK)
        total = across(high, got, apply) + across(low, got, apply)
        w_new_ref[:, at] = (w_ref[:, at].astype(F32) - total) * keep
        copies.append(pltpu.make_async_copy(w_new_ref.at[:, at], w_out.at[:, at], sems.at[i]))
        copies[-1].start()
    c_high, c_low = cols(rows_w, width), cols(rows_w + lanes_for(width), width)
    total = across(high, c_high, apply) + (across(low, c_high, apply) + across(high, c_low, apply))
    h_new_ref[...] = h_ref[...] - total.T
    copies.append(pltpu.make_async_copy(h_new_ref, h_out, sems.at[steps]))
    copies[-1].start()
    for copy in copies:
        copy.wait()


def sent_to_all(copies, axis):
    return lax.all_to_all(copies, axis, split_axis=0, concat_axis=0, tiled=True)


def on_device(hessian_inverse, weights, pruned):
    tile_rows, tile_cols = hessian_inverse.shape
    rows_w = weights.shape[0]
    n = pruned.shape[0]
    tiles = lax.axis_size("row")
    cap = 2 * n // tiles
    at = jnp.stack([lax.axis_index("row"), lax.axis_index("col")]).astype(jnp.int32)
    weights = weights.T
    listed = pruned.reshape(1, n)
    length = rows_w + 2 * lanes_for(tile_rows)
    hands = pl.pallas_call(
        pack_cols,
        out_shape=jax.ShapeDtypeStruct((8 * tiles, length // 2), BF16),
        in_specs=[VMEM, VMEM, VMEM],
        out_specs=VMEM,
        name="pack_cols",
        compiler_params=pltpu.CompilerParams(vmem_limit_bytes=GRANT),
    )(listed, hessian_inverse, weights)
    hands = sent_to_all(hands, "col")
    mine = n // tiles
    rows = pl.pallas_call(
        pack_rows,
        out_shape=jax.ShapeDtypeStruct((cap * tile_cols // 128, 128), F32),
        in_specs=[SMEM, VMEM, VMEM],
        out_specs=VMEM,
        name="pack_rows",
        compiler_params=pltpu.CompilerParams(vmem_limit_bytes=GRANT),
    )(at, listed, hessian_inverse)

    def swapped(value, mask):
        return lax.ppermute(value, "row", [(i, i ^ mask) for i in range(tiles)])

    near_rows = [rows] + [swapped(rows, 2 * m) for m in range(1, 4)]
    near_rows = jnp.stack(near_rows)
    low, high, pieces = pl.pallas_call(
        functools.partial(gather_hand, height=tile_rows, width=tile_cols),
        out_shape=(
            jax.ShapeDtypeStruct((mine // 2, length), BF16),
            jax.ShapeDtypeStruct((mine // 2, length), BF16),
            jax.ShapeDtypeStruct((tiles, 8, cap // 8 * (mine // 2)), F32),
        ),
        in_specs=[SMEM, VMEM, VMEM],
        out_specs=(VMEM, VMEM, VMEM),
        name="gather_hand",
        compiler_params=pltpu.CompilerParams(vmem_limit_bytes=GRANT),
    )(at, listed, hands)
    pieces = sent_to_all(pieces, "row")
    side = math.isqrt(tiles)

    def along_x(value, d):
        return lax.ppermute(value, "col", [(c, c // side * side + (c + d) % side) for c in range(tiles)])

    def along_y(value, d):
        return lax.ppermute(value, "col", [(c, (c + d * side) % tiles) for c in range(tiles)])

    lows = [low] + [along_x(low, d) for d in range(1, side)]
    highs = [high] + [along_y(high, d) for d in range(1, side)]
    slab = pl.pallas_call(
        functools.partial(pack_slab, width=tile_rows),
        out_shape=jax.ShapeDtypeStruct((tiles, mine // 2, n), F32),
        in_specs=[VMEM, VMEM],
        out_specs=VMEM,
        scratch_shapes=[pltpu.VMEM((n + cap, 128), F32)],
        name="pack_slab",
        compiler_params=pltpu.CompilerParams(vmem_limit_bytes=GRANT),
    )(listed, pieces)
    slab = sent_to_all(slab, "col")
    low, high = pl.pallas_call(
        join,
        out_shape=(jax.ShapeDtypeStruct((side * mine // 2, length), BF16),) * 2,
        in_specs=[VMEM] * (2 * side),
        out_specs=(VMEM, VMEM),
        name="join",
        compiler_params=pltpu.CompilerParams(vmem_limit_bytes=GRANT),
    )(*lows, *highs)
    cols = [low] + [along_y(low, d) for d in range(1, side)]
    cols += [high] + [along_x(high, d) for d in range(1, side)]
    far_rows = swapped(near_rows, 8)
    twin_near = swapped(near_rows, 1)
    slab_twin = swapped(slab, 1)
    inverse = pl.pallas_call(
        invert,
        out_shape=jax.ShapeDtypeStruct((n // BASE, n, BASE), F32),
        in_specs=[SMEM, VMEM, VMEM],
        out_specs=VMEM,
        scratch_shapes=[pltpu.VMEM((8, BASE), F32)],
        name="invert",
        compiler_params=pltpu.CompilerParams(vmem_limit_bytes=GRANT),
    )(at, slab, slab_twin)
    twin_far = swapped(far_rows, 1)
    h_new, w_new = pl.pallas_call(
        update,
        out_shape=(
            jax.ShapeDtypeStruct(hessian_inverse.shape, F32),
            jax.ShapeDtypeStruct(weights.shape, F32),
        ),
        in_specs=[SMEM] + [VMEM] * (8 + len(cols)),
        out_specs=(ANY, ANY),
        scratch_shapes=[
            pltpu.VMEM((-(-tile_cols // 128), n + cap, 128), F32),
            pltpu.VMEM(weights.shape, F32),
            pltpu.VMEM(hessian_inverse.shape, F32),
            pltpu.SemaphoreType.DMA((rows_w // BLOCK + 1,)),
        ],
        name="update",
        compiler_params=pltpu.CompilerParams(vmem_limit_bytes=GRANT),
    )(
        at, listed, inverse, near_rows, far_rows, twin_near, twin_far, *cols, hessian_inverse, weights
    )
    return h_new, w_new.T


def solution(mesh):
    specs = (P("row", "col"), P("row", "col"))

    return jax.shard_map(on_device, mesh=mesh, in_specs=(*specs, P()), out_specs=specs, check_vma=False)
```

```python
import functools
import math

import jax
import jax.numpy as jnp
from jax import lax
from jax.experimental import pallas as pl
from jax.experimental.pallas import tpu as pltpu
from jax.sharding import PartitionSpec as P


HIGH = lax.Precision.HIGHEST
F32 = jnp.float32
BF16 = jnp.bfloat16
VMEM = pl.BlockSpec(memory_space=pltpu.VMEM)
SMEM = pl.BlockSpec(memory_space=pltpu.SMEM)
ANY = pl.BlockSpec(memory_space=pl.ANY)
BASE = 128
GRANT = 24 << 20
BLOCK = 256


def across(a, b, dims, precision=None):
    return lax.dot_general(a, b, (dims, ((), ())), precision=precision, preferred_element_type=F32)


def one_hot(index, width):
    slots = index.shape[0]
    return jnp.where(index == lax.broadcasted_iota(jnp.int32, (slots, width), 1), 1.0, 0.0)


def held(pruned, tile, width, place):
    low = tile * width
    before = jnp.sum(jnp.where(pruned < low, 1, 0), axis=1, keepdims=True)
    place = place(before)
    lane = lax.broadcasted_iota(jnp.int32, (place.shape[0], pruned.shape[1]), 1)
    here = (lane == place) & (pruned >= low) & (pruned < low + width)
    return jnp.sum(jnp.where(here, pruned - low + 1, 0), axis=1, keepdims=True) - 1


def in_turn(cap):
    slot = lax.broadcasted_iota(jnp.int32, (cap, 1), 0)
    return lambda before: before + slot


def dealt(before, tiles, slots):
    slot = lax.broadcasted_iota(jnp.int32, (tiles * 2 * slots, 1), 0)
    hand, second, turn = slot // (2 * slots), slot // slots % 2, slot % slots
    return hand, second, (before - hand + tiles - 1) // tiles + turn


def lanes_for(width):
    return -(-width // 128) * 128


def pack_rows(at_ref, pruned_ref, h_ref, rows_ref):
    height, width = h_ref.shape
    cap = rows_ref.shape[0] * 128 // width
    pick = one_hot(held(pruned_ref[...], at_ref[0], height, in_turn(cap)), height)
    rows_ref[...] = strips_of(across(pick, h_ref[...], ((1,), (0,)), HIGH))


def strips_of(rows):
    count, width = rows.shape
    full = width // 128 * 128
    rest = width - full
    groups = 128 // rest
    each = count // groups
    strips = [rows[:, j : j + 128] for j in range(0, full, 128)]
    strips.append(jnp.concatenate([rows[each * i : each * i + each, full:] for i in range(groups)], axis=1))
    return jnp.concatenate(strips, axis=0)


def place_strips(ref, start, packed, count, width):
    full = width // 128
    rest = width - 128 * full
    each = count * rest // 128
    for j in range(full):
        ref[j, pl.ds(start, count), :] = packed[count * j : count * j + count]
    last = packed[count * full :]
    for i in range(128 // rest):
        ref[full, pl.ds(start + each * i, each), 0:rest] = last[:, rest * i : rest * i + rest]


def pack_cols(pruned_ref, h_hbm, w_hbm, out_ref, h_ref, w_ref, sems):
    slots, half = out_ref.shape
    copies = [
        pltpu.make_async_copy(h_hbm, h_ref, sems.at[0]),
        pltpu.make_async_copy(w_hbm.at[:, half:], w_ref.at[:, half:], sems.at[1]),
        pltpu.make_async_copy(w_hbm.at[:, :half], w_ref.at[:, :half], sems.at[2]),
    ]
    for copy in copies:
        copy.start()
    pruned = pruned_ref[...]
    width = h_ref.shape[1]
    tiles = slots // 8
    pick = one_hot(held(pruned, lax.axis_index("col"), width, lambda before: dealt_places(before, tiles, 4)), width)
    picked = pick.astype(BF16)
    copies[0].wait()
    c = across(pick, h_ref[...], ((1,), (1,)), HIGH)
    c_high = c.astype(BF16).astype(F32)
    copies[1].wait()
    last = across(picked, w_ref[:, half:], ((1,), (0,)))
    spare = jnp.zeros((slots, lanes_for(width) - width), F32)
    last = jnp.concatenate([last, c_high, spare, c - c_high, spare], axis=1)
    second = lax.broadcasted_iota(jnp.int32, (slots, 1), 0) // 4 % 2
    copies[2].wait()
    first = across(picked, w_ref[:, :half], ((1,), (0,)))
    out_ref[...] = jnp.where(second == 1, last, first).astype(BF16)


def dealt_places(before, tiles, slots):
    hand, _, turn = dealt(before, tiles, slots)
    return hand + tiles * turn


def gather_hand(at_ref, pruned_ref, got_ref, low_ref, high_ref, piece_ref, *, height, width):
    pruned = pruned_ref[...]
    slots, half = got_ref.shape
    tiles = piece_ref.shape[0]
    mine = pruned.shape[1] // tiles
    slot = lax.broadcasted_iota(jnp.int32, (slots, 1), 0)
    tile, second, turn = slot // 8, slot // 4 % 2, slot % 4
    before = jnp.sum(jnp.where(pruned < tile * width, 1, 0), axis=1, keepdims=True)
    after = jnp.sum(jnp.where(pruned < tile * width + width, 1, 0), axis=1, keepdims=True)
    hand = at_ref[1]
    turn = (before - hand + tiles - 1) // tiles + turn
    turn = jnp.where(hand + tiles * turn < after, turn, -1)
    got = got_ref[...]
    parts = [
        across(one_hot(jnp.where(second == part, turn, -1), mine).astype(BF16), got, ((0,), (0,)))
        for part in range(2)
    ]
    wide = lanes_for(height)
    c = parts[1][:, half - 2 * wide : half - 2 * wide + height] + parts[1][:, half - wide : half - wide + height]
    cap = 2 * mine
    pick = one_hot(held(pruned, at_ref[0], height, in_turn(cap)), height)
    piece = across(pick, c, ((1,), (1,)), HIGH)
    for core in range(2):
        part = piece[:, mine // 2 * core : mine // 2 * (core + 1)]
        part = jnp.concatenate([part[8 * i : 8 * i + 8] for i in range(cap // 8)], axis=1)
        for d in range(core, tiles, 2):
            piece_ref[d] = part
    for part in range(2):
        lanes = slice(half * part, half * part + half)
        low_ref[:, lanes] = parts[part][: mine // 2].astype(BF16)
        high_ref[:, lanes] = parts[part][mine // 2 :].astype(BF16)


def join(*refs):
    count = (len(refs) - 2) // 2
    for path in range(2):
        out = refs[2 * count + path]
        rows = out.shape[0] // count
        for d in range(count):
            out[rows * d : rows * d + rows, :] = refs[count * path + d][...]


def pack_slab(pruned_ref, got_ref, out_ref, slab_ref, *, width):
    tiles, mine, n = out_ref.shape
    groups = got_ref.shape[2] // mine
    first = first_places(pruned_ref[...], tiles, width)
    for t in range(tiles):
        got = got_ref[t]
        for i in range(groups):
            slab_ref[pl.ds(first[t] + 8 * i, 8), 0:mine] = got[:, mine * i : mine * i + mine]
    slab = slab_ref[0:n, :].T[0:mine, :]
    for d in range(tiles):
        out_ref[d] = slab


def first_places(pruned, tiles, width):
    return [jnp.sum(jnp.where(pruned < t * width, 1, 0)) for t in range(tiles)]


def spread(v, i):
    return jnp.broadcast_to(v[i : i + 1, :], v.shape)


def base_factors(tiles, zero, work):
    width = tiles[0].shape[1]
    lane = lax.broadcasted_iota(jnp.int32, (8, width), 1)
    sub = lax.broadcasted_iota(jnp.int32, (8, width), 0)
    tiles = list(tiles)
    count = len(tiles)
    lower, scaled = [], []
    for t in range(count):
        q = 8 * t
        own = tiles[t]
        cols = [jnp.broadcast_to(own[:, q + j : q + j + 1], (8, width)) + zero for j in range(8)]
        here = (lane >= q) & (lane < q + 8)
        known = lane < q + 8
        panel = jnp.where(here, jnp.where(lane - q == sub, 1.0, 0.0), own)
        lower.append(jnp.where(known, panel, 0.0))
        for j in range(0, 8, 2):
            k = j + 1
            a, b, b2, c = spread(cols[j], j), spread(cols[k], j), spread(cols[j], k), spread(cols[k], k)
            r = 1.0 / (a * c - b * b2)
            i00, i01, i10, i11 = c * r, -(b * r), -(b2 * r), a * r
            is_j, is_k = sub == j, sub == k
            f_j = jnp.where(is_j, -i00, jnp.where(is_k, -i10, cols[j] * i00 + cols[k] * i10))
            f_k = jnp.where(is_j, -i01, jnp.where(is_k, -i11, cols[j] * i01 + cols[k] * i11))
            pivot = is_j | is_k

            def swept(v):
                return jnp.where(pivot, 0.0, v) - (f_j * spread(v, j) + f_k * spread(v, k))

            for m in range(j + 2, 8):
                cols[m] = swept(cols[m])
            panel = swept(panel)
        scaled.append(jnp.where(known, panel, 0.0))
        rows = [spread(panel, j) for j in range(8)]
        if work:
            work.pop(0)()
        for s in range(t + 1, count):
            v = tiles[s]
            p = [jnp.broadcast_to(v[:, q + j : q + j + 1], (8, width)) * rows[j] for j in range(8)]
            total = ((p[0] + p[1]) + (p[2] + p[3])) + ((p[4] + p[5]) + (p[6] + p[7]))
            tiles[s] = jnp.where(here, 0.0, v) - total
    return jnp.concatenate(lower, axis=0), jnp.concatenate(scaled, axis=0)


def invert(at_ref, own_ref, other_ref, out_ref, zero_ref):
    tiles, half, n = own_ref.shape
    low_is_own = at_ref[0] % 2 == 0
    for t in range(tiles):
        own, other = own_ref[t], other_ref[t]
        low, high = jnp.where(low_is_own, own, other), jnp.where(low_is_own, other, own)
        for j in range(n // BASE):
            lanes = slice(BASE * j, BASE * j + BASE)
            out_ref[j, pl.ds(t, half, stride=tiles), :] = low[:, lanes]
            out_ref[j, pl.ds(t + half * tiles, half, stride=tiles), :] = high[:, lanes]
    zero_ref[...] = jnp.zeros_like(zero_ref)
    zero = zero_ref[...]
    blocks = n // BASE
    work = []
    for k in range(blocks):
        own = slice(BASE * k, BASE * k + BASE)
        diagonal = out_ref[k, own, :]
        lower, scaled = base_factors([diagonal[s : s + 8] for s in range(0, BASE, 8)], zero, work)
        while work:
            work.pop(0)()
        base = across(lower, scaled, ((0,), (0,)), HIGH)
        rows = {k: base}
        cols = [out_ref[k, BASE * r : BASE * r + BASE, :] for r in range(blocks)]
        out_ref[k, own, :] = base

        def row(c, own=own, rows=rows, base=base):
            rows[c] = across(base, out_ref[c, own, :], ((1,), (0,)), HIGH)
            out_ref[c, own, :] = rows[c]

        def product(r, c, k=k, rows=rows, cols=cols):
            at = (c, slice(BASE * r, BASE * r + BASE))
            total = across(cols[r], rows[c], ((1,), (0,)), HIGH)
            out_ref[at] = -total if c == k else out_ref[at] - total

        following = (k + 1) % blocks
        if k + 1 < blocks:
            row(following)
            product(following, following)
        for c in [(k + i) % blocks for i in range(1, blocks)]:
            if c != following or k + 1 == blocks:
                work.append(functools.partial(row, c))
        for c in [(k + i) % blocks for i in range(1, blocks + 1)]:
            for r in [(k + i) % blocks for i in range(1, blocks)]:
                if not r == c == k + 1:
                    work.append(functools.partial(product, r, c))
    while work:
        work.pop(0)()


def update(at_ref, pruned_ref, inv_ref, near_ref, far_ref, twin_near_ref, twin_far_ref, *refs):
    blocks, (h_ref, w_ref, h_out, w_out, panel_ref, w_new_ref, h_new_ref, sems) = refs[:-8], refs[-8:]
    strips, n, _ = inv_ref.shape
    width = h_ref.shape[1]
    tiles = 4 * near_ref.shape[0]
    first = first_places(pruned_ref[...], tiles, h_ref.shape[0])
    cap = 2 * n // tiles
    side = len(blocks) // 2
    rows_w = w_ref.shape[1]
    steps = rows_w // BLOCK
    core, z = at_ref[0] % 2, at_ref[0] // 2
    near = near_ref.shape[0]
    for t in range(tiles):
        apart = (t // 2) ^ z
        of = apart % near
        own = jnp.where(apart < near, near_ref[of], far_ref[of])
        twin = jnp.where(apart < near, twin_near_ref[of], twin_far_ref[of])
        place_strips(panel_ref, first[t], jnp.where(core == t % 2, own, twin), cap, width)
    panel = jnp.concatenate([panel_ref[j, 0:n, :] for j in range(panel_ref.shape[0])], axis=1).T[:width, :]
    x, y = at_ref[1] % side, at_ref[1] // side
    hands = []
    for path in range(2):
        for far in range(side):
            for near in range(side):
                dx, dy = (near, far) if path == 0 else (far, near)
                hand = (y + side - dy) % side * side + (x + side - dx) % side
                hands.append(hand + path * (n // 2))
    inverse = jnp.concatenate(
        [
            jnp.concatenate([inv_ref[j, pl.ds(h, n // tiles // 2, stride=tiles), :] for h in hands], axis=0)
            for j in range(strips)
        ],
        axis=1,
    )
    solved = across(panel, inverse, ((1,), (1,)), HIGH)
    high = solved.astype(BF16)
    low = (solved - high.astype(F32)).astype(BF16)
    unit = lax.broadcasted_iota(jnp.int32, (width, n), 0) + at_ref[1] * width
    keep = 1.0 - jnp.sum(jnp.where(unit == pruned_ref[...], 1.0, 0.0), axis=1, keepdims=True)
    apply = ((1,), (0,))

    def cols(start, size):
        return jnp.concatenate([b[:, start : start + size] for b in blocks], axis=0)

    copies = []
    for i in range(steps):
        at = slice(BLOCK * i, BLOCK * i + BLOCK)
        got = cols(BLOCK * i, BLOCK)
        total = across(high, got, apply) + across(low, got, apply)
        w_new_ref[:, at] = (w_ref[:, at].astype(F32) - total) * keep
        copies.append(pltpu.make_async_copy(w_new_ref.at[:, at], w_out.at[:, at], sems.at[i]))
        copies[-1].start()
    c_high, c_low = cols(rows_w, width), cols(rows_w + lanes_for(width), width)
    total = across(high, c_high, apply) + (across(low, c_high, apply) + across(high, c_low, apply))
    h_new_ref[...] = h_ref[...] - total.T
    copies.append(pltpu.make_async_copy(h_new_ref, h_out, sems.at[steps]))
    copies[-1].start()
    for copy in copies:
        copy.wait()


def sent_to_all(copies, axis):
    return lax.all_to_all(copies, axis, split_axis=0, concat_axis=0, tiled=True)


def on_device(hessian_inverse, weights, pruned):
    tile_rows, tile_cols = hessian_inverse.shape
    rows_w = weights.shape[0]
    n = pruned.shape[0]
    tiles = lax.axis_size("row")
    cap = 2 * n // tiles
    at = jnp.stack([lax.axis_index("row"), lax.axis_index("col")]).astype(jnp.int32)
    weights = weights.T
    listed = pruned.reshape(1, n)
    length = rows_w + 2 * lanes_for(tile_rows)
    hands = pl.pallas_call(
        pack_cols,
        out_shape=jax.ShapeDtypeStruct((8 * tiles, length // 2), BF16),
        in_specs=[VMEM, ANY, ANY],
        out_specs=VMEM,
        scratch_shapes=[
            pltpu.VMEM(hessian_inverse.shape, F32),
            pltpu.VMEM(weights.shape, BF16),
            pltpu.SemaphoreType.DMA((3,)),
        ],
        name="pack_cols",
    )(listed, hessian_inverse, weights)
    hands = sent_to_all(hands, "col")
    mine = n // tiles
    rows = pl.pallas_call(
        pack_rows,
        out_shape=jax.ShapeDtypeStruct((cap * tile_cols // 128, 128), F32),
        in_specs=[SMEM, VMEM, VMEM],
        out_specs=VMEM,
        name="pack_rows",
        compiler_params=pltpu.CompilerParams(vmem_limit_bytes=GRANT),
    )(at, listed, hessian_inverse)

    def swapped(value, mask):
        return lax.ppermute(value, "row", [(i, i ^ mask) for i in range(tiles)])

    near_rows = [rows] + [swapped(rows, 2 * m) for m in range(1, 4)]
    near_rows = jnp.stack(near_rows)
    low, high, pieces = pl.pallas_call(
        functools.partial(gather_hand, height=tile_rows, width=tile_cols),
        out_shape=(
            jax.ShapeDtypeStruct((mine // 2, length), BF16),
            jax.ShapeDtypeStruct((mine // 2, length), BF16),
            jax.ShapeDtypeStruct((tiles, 8, cap // 8 * (mine // 2)), F32),
        ),
        in_specs=[SMEM, VMEM, VMEM],
        out_specs=(VMEM, VMEM, VMEM),
        name="gather_hand",
        compiler_params=pltpu.CompilerParams(vmem_limit_bytes=GRANT),
    )(at, listed, hands)
    pieces = sent_to_all(pieces, "row")
    side = math.isqrt(tiles)

    def along_x(value, d):
        return lax.ppermute(value, "col", [(c, c // side * side + (c + d) % side) for c in range(tiles)])

    def along_y(value, d):
        return lax.ppermute(value, "col", [(c, (c + d * side) % tiles) for c in range(tiles)])

    lows = [low] + [along_x(low, d) for d in range(1, side)]
    highs = [high] + [along_y(high, d) for d in range(1, side)]
    slab = pl.pallas_call(
        functools.partial(pack_slab, width=tile_rows),
        out_shape=jax.ShapeDtypeStruct((tiles, mine // 2, n), F32),
        in_specs=[VMEM, VMEM],
        out_specs=VMEM,
        scratch_shapes=[pltpu.VMEM((n + cap, 128), F32)],
        name="pack_slab",
        compiler_params=pltpu.CompilerParams(vmem_limit_bytes=GRANT),
    )(listed, pieces)
    slab = sent_to_all(slab, "col")
    low, high = pl.pallas_call(
        join,
        out_shape=(jax.ShapeDtypeStruct((side * mine // 2, length), BF16),) * 2,
        in_specs=[VMEM] * (2 * side),
        out_specs=(VMEM, VMEM),
        name="join",
        compiler_params=pltpu.CompilerParams(vmem_limit_bytes=GRANT),
    )(*lows, *highs)
    cols = [low] + [along_y(low, d) for d in range(1, side)]
    cols += [high] + [along_x(high, d) for d in range(1, side)]
    far_rows = swapped(near_rows, 8)
    twin_near = swapped(near_rows, 1)
    slab_twin = swapped(slab, 1)
    inverse = pl.pallas_call(
        invert,
        out_shape=jax.ShapeDtypeStruct((n // BASE, n, BASE), F32),
        in_specs=[SMEM, VMEM, VMEM],
        out_specs=VMEM,
        scratch_shapes=[pltpu.VMEM((8, BASE), F32)],
        name="invert",
        compiler_params=pltpu.CompilerParams(vmem_limit_bytes=GRANT),
    )(at, slab, slab_twin)
    twin_far = swapped(far_rows, 1)
    h_new, w_new = pl.pallas_call(
        update,
        out_shape=(
            jax.ShapeDtypeStruct(hessian_inverse.shape, F32),
            jax.ShapeDtypeStruct(weights.shape, F32),
        ),
        in_specs=[SMEM] + [VMEM] * (8 + len(cols)),
        out_specs=(ANY, ANY),
        scratch_shapes=[
            pltpu.VMEM((-(-tile_cols // 128), n + cap, 128), F32),
            pltpu.VMEM(weights.shape, F32),
            pltpu.VMEM(hessian_inverse.shape, F32),
            pltpu.SemaphoreType.DMA((rows_w // BLOCK + 1,)),
        ],
        name="update",
        compiler_params=pltpu.CompilerParams(vmem_limit_bytes=GRANT),
    )(
        at, listed, inverse, near_rows, far_rows, twin_near, twin_far, *cols, hessian_inverse, weights
    )
    return h_new, w_new.T


def solution(mesh):
    specs = (P("row", "col"), P("row", "col"))

    return jax.shard_map(on_device, mesh=mesh, in_specs=(*specs, P()), out_specs=specs, check_vma=False)
```
